512 devices in a mesh: dom: 32 (over y, x_hi, core), band: 16 (over z, x_lo).
Axes of the slice: x: 4 (x_hi: 2, x_lo: 2; x = x_hi * 2 + x_lo), y: 8, z: 8, core: 2. Of those that a mesh axis runs over, the one named last changes fastest.
Arguments:
- psi: float32 [512, 192, 512], P('band', 'dom'), may hold values from -40 to 40, as said below
- potential: float32 [192, 512], P('dom'), may hold values from -3 to 1
Outputs:
- filtered_basis: float32 [512, 192, 512], P('band', 'dom')
The draws below stay inside these ranges and needn't reach their ends.
Inputs may be any that keep to these rules, and one draw needn't show every extreme that they name: `psi`: real-valued band functions.
All inputs are finite; a program needn't handle non-finite values.
Results may differ from the reference program's by a relative error of at most 0.0002.
Values sent between devices are 32-bit elements; how exact they have to be, the bound alone decides.
No kernel may reach another device: no remote copies, remote signals or barrier semaphores. Data moves between devices by JAX's collectives and lax.ppermute only.
A program may use at most 64 MiB of HBM per device.

```python
import math
import jax
import jax.numpy as jnp
from jax import lax

NB = 512
LX = 32
LY = 16
DEG = 4
NZ = 192
NPTS = 98304


def draw_psi(key, part):
    key_base, key_band, key_layer = jax.random.split(key, 3)
    upper_log = 0.5 * math.log(10.0)
    band_scale = jnp.exp(jax.random.uniform(key_band, (NB, 1, 1), jnp.float32, 0.0, upper_log))
    layer_scale = jnp.exp(jax.random.uniform(key_layer, (1, NZ, 1), jnp.float32, 0.0, upper_log))
    base = jnp.clip(jax.random.normal(key_base, (NB, NZ, LX * LY), jnp.float32), -4.0, 4.0)
    return base * band_scale * layer_scale


def steps_of(own_key, extent, cuts, smallest, top_value):
    factor_of = 1.0
    for position, parts in cuts:
        draws = jax.random.uniform(jax.random.fold_in(jax.random.fold_in(own_key, 6), position), (parts,), jnp.float32, smallest / len(cuts), top_value / len(cuts))
        factor_of = factor_of * jnp.repeat(jnp.exp(draws), extent[position] // parts).reshape((-1,) + (1,) * (len(extent) - 1 - position))
    return factor_of


def setup_inputs(seed: int = 0) -> dict:
    keys = jax.random.split(jax.random.key(seed), 3)
    psi = draw_psi(jax.random.fold_in(keys[2], 71), 0)
    potential = jnp.clip(-3.0 + 4.0 * jax.random.uniform(keys[1], (NZ, LX * LY), jnp.float32) ** steps_of(keys[1], (NZ, LX * LY), ((0, 32),), -0.2, 0.2), -3.0, 1.0)
    return dict(psi=psi, potential=potential)


COEF = (-5369.0 / 1800.0, 12.0 / 7.0, -15.0 / 56.0, 10.0 / 189.0, -1.0 / 112.0, 2.0 / 1925.0, -1.0 / 16632.0)
INV_SPACING2 = 4.0
CENTRE = 24.0
HALF_WIDTH = 20.0

def laplace(values):
    nbands, depth, flat = values.shape
    volume = values.reshape(nbands, depth, LY, LX)
    padded = jnp.pad(volume, ((0, 0), (6, 6), (0, 0), (0, 0)))
    summed = 3.0 * COEF[0] * volume
    for step in range(1, 7):
        beside_all = jnp.roll(volume, step, 3) + jnp.roll(volume, -step, 3)
        beside_all = beside_all + jnp.roll(volume, step, 2) + jnp.roll(volume, -step, 2)
        beside_all = beside_all + padded[:, 6 + step:6 + step + depth] + padded[:, 6 - step:6 - step + depth]
        summed = summed + COEF[step] * beside_all
    return (INV_SPACING2 * summed).reshape(nbands, depth, flat)

def hamiltonian(values, potential):
    return -0.5 * laplace(values) + potential[None] * values

def chebyshev(start, potential):
    previous = start
    current = (hamiltonian(start, potential) - CENTRE * start) / HALF_WIDTH
    for degree in range(1, DEG):
        following = 2.0 * (hamiltonian(current, potential) - CENTRE * current) / HALF_WIDTH - previous
        previous, current = (current, following)
    return current

def reference(psi, potential):
    blocks = psi.reshape(8, NB // 8, NZ, LX * LY)
    filtered = lax.map(lambda block: chebyshev(block, potential), blocks)
    flatrows = filtered.reshape(NB, NPTS)
    gram = jnp.dot(flatrows.astype(jnp.float32), flatrows.T.astype(jnp.float32), precision=lax.Precision.HIGHEST, preferred_element_type=jnp.float32) / NPTS
    lower = jnp.linalg.cholesky(gram)
    solved = lax.linalg.triangular_solve(lower, flatrows, left_side=True, lower=True)
    return solved.reshape(NB, NZ, LX * LY)
```

```python
import jax
import jax.numpy as jnp
import numpy as np
from jax import lax
from jax.experimental import pallas as pl
from jax.experimental.pallas import tpu as pltpu
from jax.sharding import PartitionSpec as P

NB = 512
LX = 32
LY = 16
NZ = 192
CELLS = LX * LY
NPTS = NZ * CELLS
DEG = 4
DOM = 32
BAND = 16
TILE = NB // BAND
DEPTH = NZ // DOM
LANES = 128
ALL = ("band", "dom")

COEF = (
    -5369.0 / 1800.0,
    12.0 / 7.0,
    -15.0 / 56.0,
    10.0 / 189.0,
    -1.0 / 112.0,
    2.0 / 1925.0,
    -1.0 / 16632.0,
)
INV_SPACING2 = 4.0
CENTRE = 24.0
HALF_WIDTH = 20.0

HIGHEST = lax.Precision.HIGHEST
f32 = jnp.float32
bf16 = jnp.bfloat16


def split_constant(matrix):
    pieces = []
    rest = matrix.astype(np.float64)
    for _ in range(3):
        piece = rest.astype(np.float32).astype(bf16)
        pieces.append(piece)
        rest = rest - piece.astype(np.float64)
    return pieces


def plane_matrix():
    out = np.zeros((CELLS, CELLS))
    scale = -0.5 * INV_SPACING2 / HALF_WIDTH
    for y in range(LY):
        for x in range(LX):
            row = y * LX + x
            out[row, row] += scale * 3.0 * COEF[0] - CENTRE / HALF_WIDTH
            for k in range(1, 7):
                for step in (k, -k):
                    out[row, y * LX + (x + step) % LX] += scale * COEF[k]
                    out[row, (y + step) % LY * LX + x] += scale * COEF[k]
    return out


def layer_matrix():
    out = np.zeros((NZ, NZ))
    scale = -0.5 * INV_SPACING2 / HALF_WIDTH
    for k in range(1, 7):
        out += scale * COEF[k] * (np.eye(NZ, k=k) + np.eye(NZ, k=-k))
    return out


def split_value(value):
    high = value.astype(bf16)
    rest = value - high.astype(f32)
    middle = rest.astype(bf16)
    low = (rest - middle.astype(f32)).astype(bf16)
    return high, middle, low


def dot_split(left, right):
    def dot(a, b):
        return jnp.dot(a, b, preferred_element_type=f32)

    small = dot(left[0], right[2]) + dot(left[1], right[1]) + dot(left[2], right[0])
    return (small + (dot(left[0], right[1]) + dot(left[1], right[0]))) + dot(left[0], right[0])


def pack_kernel(psi, potential, out):
    for layer in range(DEPTH):
        for quarter in range(4):
            lanes = slice(quarter * LANES, (quarter + 1) * LANES)
            row = layer * 8 + quarter
            out[pl.ds(row, TILE, stride=8 * DEPTH), :] = psi[layer, :, lanes]
            out[pl.ds(row + 4, TILE, stride=8 * DEPTH), :] = jnp.broadcast_to(
                potential[layer : layer + 1, lanes] * (1.0 / HALF_WIDTH), (TILE, LANES)
            )


def filter_kernel(rows, m0, m1, m2, v0, v1, v2, out, scratch):
    start = jnp.concatenate([rows[pl.ds(q, NZ, stride=8), :] for q in range(4)], axis=1)
    potential = jnp.concatenate([rows[pl.ds(4 + q, NZ, stride=8), :] for q in range(4)], axis=1)
    plane = (m0[...], m1[...], m2[...])
    layers = (v0[...], v1[...], v2[...])

    def apply(values):
        pieces = split_value(values)
        return dot_split(pieces, plane) + dot_split(layers, pieces) + potential * values

    previous = start
    current = apply(start)
    for _ in range(1, DEG):
        previous, current = current, 2.0 * apply(current) - previous
    norm = jnp.sum(jnp.sum(current * current, axis=0, keepdims=True), axis=1, keepdims=True) * (
        1.0 / NPTS
    )
    for quarter in range(4):
        scratch[quarter * NZ : (quarter + 1) * NZ, :] = current[
            :, quarter * LANES : (quarter + 1) * LANES
        ]
    lane = lax.broadcasted_iota(jnp.int32, (DOM, LANES), 1)
    norms = jnp.broadcast_to(norm, (DOM, LANES))
    for piece in range(BAND):
        first = scratch[pl.ds((piece % 4) * NZ + piece // 4, DOM, stride=DEPTH), :]
        half = piece // 2
        second = scratch[pl.ds((half % 4) * NZ + 4 + half // 4, DOM, stride=DEPTH), :]
        valid = lane < 64 if piece % 2 == 0 else lane >= 64
        out[pl.ds(piece * 2 * DOM, DOM, stride=2), :] = first
        out[pl.ds(piece * 2 * DOM + 1, DOM, stride=2), :] = jnp.where(valid, second, norms)


def points_of(rows, odd):
    first = rows[pl.ds(0, NB, stride=2), :]
    second = rows[pl.ds(1, NB, stride=2), :]
    upper = (lax.broadcasted_iota(jnp.int32, (NB, LANES), 1) >= 64).astype(jnp.int32)
    return first, jnp.where(upper == odd, second, 0.0), second


def dot_nt(a, b):
    return lax.dot_general(
        a, b, (((1,), (1,)), ((), ())), precision=HIGHEST, preferred_element_type=f32
    )


def dot_nn(a, b):
    return jnp.dot(a, b, precision=HIGHEST, preferred_element_type=f32)


def gram_kernel(odd, rows, out):
    first, second, _ = points_of(rows, odd[0])
    points = jnp.concatenate([first, second], axis=1)
    low, high = points[:256], points[256:]
    row = lax.broadcasted_iota(jnp.int32, (256, 256), 0)
    col = lax.broadcasted_iota(jnp.int32, (256, 256), 1)
    folded = jnp.where(col <= row, dot_nt(low, low), dot_nt(high, high))
    below = dot_nt(high, low)
    out[0:256, :] = folded[:, :LANES]
    out[256:512, :] = folded[:, LANES:]
    out[512:768, :] = below[:, :LANES]
    out[768:1024, :] = below[:, LANES:]


def sum_kernel(parts, out):
    total = jnp.sum(parts[...].reshape(8, 16, 8, LANES), axis=0)
    total = jnp.sum(total, axis=0)
    total = total + pltpu.roll(total, 4, 0)
    total = (total + pltpu.roll(total, 2, 0)) * (1.0 / NPTS)
    out[...] = jnp.broadcast_to(total[None], (NB // 4, 8, LANES)).reshape(2 * NB, LANES)


def invert_block(block, inverse):
    full = (8, LANES)
    row = lax.broadcasted_iota(jnp.int32, (LANES, LANES), 0)
    col = lax.broadcasted_iota(jnp.int32, (LANES, LANES), 1)
    inverse[...] = jnp.where(row == col, 1.0, 0.0)
    sub = lax.broadcasted_iota(jnp.int32, full, 0)
    for panel in range(16):
        here = slice(8 * panel, 8 * panel + 8)
        v = block[here, :]
        w = inverse[here, :]
        cols = [
            jnp.broadcast_to(v[:, 8 * panel + t : 8 * panel + t + 1], full) for t in range(8)
        ]
        e = [[None] * 8 for _ in range(8)]
        for t in range(8):
            for s in range(t, 8):
                e[s][t] = jnp.broadcast_to(cols[t][s : s + 1, :], full)
        inv = [None] * 8
        for t in range(8):
            inv[t] = lax.rsqrt(e[t][t])
            for s in range(t + 1, 8):
                e[s][t] = e[s][t] * inv[t]
            for u in range(t + 1, 8):
                for s in range(u, 8):
                    e[s][u] = e[s][u] - e[s][t] * e[u][t]
        ys, zs = [], []
        for s in range(8):
            y = jnp.broadcast_to(v[s : s + 1, :], full)
            z = jnp.broadcast_to(w[s : s + 1, :], full)
            for u in range(s):
                y = y - e[s][u] * ys[u]
                z = z - e[s][u] * zs[u]
            ys.append(y * inv[s])
            zs.append(z * inv[s])
        done = zs[0]
        for s in range(1, 8):
            done = jnp.where(sub == s, zs[s], done)
        inverse[here, :] = done
        if panel == 15:
            break
        for s in reversed(range(8)):
            y, z = ys[s], zs[s]
            for u in range(s + 1, 8):
                y = y - e[u][s] * ys[u]
                z = z - e[u][s] * zs[u]
            ys[s], zs[s] = y * inv[s], z * inv[s]
        for q in range(panel + 1, 16):
            there = slice(8 * q, 8 * q + 8)
            d = block[there, :]
            i = inverse[there, :]
            for t in range(8):
                c = jnp.broadcast_to(block[there, 8 * panel + t : 8 * panel + t + 1], full)
                d = d - c * ys[t]
                i = i - c * zs[t]
            block[there, :] = d
            inverse[there, :] = i


def solve_kernel(odd, gram, rows, out, s_ref, x_ref, block, inverse):
    first, second, raw = points_of(rows, odd[0])
    x_ref[:, :LANES] = first
    x_ref[:, LANES:] = second
    norms = jnp.where(odd[0] == 0, raw[256:, LANES - 1 : LANES], raw[256:, 0:1])
    folded = jnp.concatenate([gram[0:256, :], gram[256:512, :]], axis=1)
    flipped = folded.T
    row = lax.broadcasted_iota(jnp.int32, (256, 256), 0)
    col = lax.broadcasted_iota(jnp.int32, (256, 256), 1)
    s_ref[:256, :256] = jnp.where(col <= row, folded, flipped)
    s_ref[256:, 256:] = jnp.where(
        col == row, jnp.broadcast_to(norms, (256, 256)), jnp.where(col > row, folded, flipped)
    )
    s_ref[256:, :LANES] = gram[512:768, :]
    s_ref[256:, LANES:256] = gram[768:1024, :]
    for j in range(4):
        here = slice(j * LANES, (j + 1) * LANES)
        rest = slice((j + 1) * LANES, NB)
        block[...] = s_ref[here, here]
        invert_block(block, inverse)
        factor_inverse = inverse[...]
        solved = dot_nn(factor_inverse, x_ref[here, :])
        x_ref[here, :] = solved
        if j < 3:
            panel = dot_nt(s_ref[rest, here], factor_inverse)
            x_ref[rest, :] = x_ref[rest, :] - dot_nn(panel, solved)
            s_ref[rest, rest] = s_ref[rest, rest] - dot_nt(panel, panel)
    for tile in range(BAND):
        at = tile * TILE
        out[tile * 48 : tile * 48 + 32, :] = x_ref[at : at + TILE, :LANES]
        out[tile * 48 + 32 : tile * 48 + 48, :] = x_ref[at : at + 16, LANES:] + pltpu.roll(
            x_ref[at + 16 : at + 32, LANES:], 64, 1
        )


def unpack_kernel(rows, out):
    for piece in range(BAND):
        quarter = piece % 4
        out[piece // 4, :, quarter * LANES : (quarter + 1) * LANES] = rows[
            piece * 48 : piece * 48 + 32, :
        ]
    lower = lax.broadcasted_iota(jnp.int32, (16, LANES), 1) < 64
    for half in range(8):
        lanes = slice((half % 4) * LANES, (half % 4 + 1) * LANES)
        even = rows[2 * half * 48 + 32 : 2 * half * 48 + 48, :]
        odd = rows[(2 * half + 1) * 48 + 32 : (2 * half + 1) * 48 + 48, :]
        out[4 + half // 4, 0:16, lanes] = jnp.where(lower, even, odd)
        out[4 + half // 4, 16:32, lanes] = pltpu.roll(jnp.where(lower, odd, even), 64, 1)


def whole():
    return pl.BlockSpec(memory_space=pltpu.VMEM)


def scalar():
    return pl.BlockSpec(memory_space=pltpu.SMEM)


def call(kernel, name, shape, specs, scratch=()):
    return pl.pallas_call(
        kernel,
        name=name,
        out_shape=jax.ShapeDtypeStruct(shape, f32),
        in_specs=specs,
        out_specs=whole(),
        scratch_shapes=list(scratch),
        compiler_params=pltpu.CompilerParams(vmem_limit_bytes=48 << 20),
    )


def do_pack(psi, potential):
    return call(pack_kernel, "pack", (TILE * 8 * DEPTH, LANES), [whole()] * 2)(psi, potential)


def do_filter(rows):
    constants = [jnp.asarray(p) for p in split_constant(plane_matrix())]
    constants += [jnp.asarray(p) for p in split_constant(layer_matrix())]
    return call(
        filter_kernel, "filter", (2 * NB, LANES), [whole()] * 7, [pltpu.VMEM((4 * NZ, LANES), f32)]
    )(rows, *constants)


def do_gram(odd, rows):
    return call(gram_kernel, "gram", (2 * NB, LANES), [scalar(), whole()])(odd, rows)


def do_sum(parts):
    return call(sum_kernel, "sum", (2 * NB, LANES), [whole()])(parts)


def do_solve(odd, gram, rows):
    return call(
        solve_kernel,
        "solve",
        (BAND * 48, LANES),
        [scalar(), whole(), whole()],
        [
            pltpu.VMEM((NB, NB), f32),
            pltpu.VMEM((NB, 2 * LANES), f32),
            pltpu.VMEM((LANES, LANES), f32),
            pltpu.VMEM((LANES, LANES), f32),
        ],
    )(odd, gram, rows)


def do_unpack(rows):
    return call(unpack_kernel, "unpack", (DEPTH, TILE, CELLS), [whole()])(rows)


def exchange(rows, axis, parts):
    shaped = rows.reshape(parts, rows.shape[0] // parts, LANES)
    return lax.all_to_all(shaped, axis, 0, 0).reshape(rows.shape)


def shards(psi, potential):
    odd = (lax.axis_index("band") % 2).astype(jnp.int32).reshape(1)
    bands = exchange(do_pack(jnp.transpose(psi, (1, 0, 2)), potential), "dom", DOM)
    points = exchange(do_filter(bands), ALL, NB)
    parts = exchange(do_gram(odd, points), ALL, NB)
    gram = exchange(do_sum(parts), ALL, NB)
    result = exchange(do_solve(odd, gram, points), "band", BAND)
    return jnp.transpose(do_unpack(result), (1, 0, 2))


def solution(mesh):
    placed = (P("band", "dom", None), P("dom", None))
    return jax.shard_map(
        shards, mesh=mesh, in_specs=placed, out_specs=P("band", "dom", None), check_vma=False
    )
```

```python
import jax
import jax.numpy as jnp
import numpy as np
from jax import lax
from jax.experimental import pallas as pl
from jax.experimental.pallas import tpu as pltpu
from jax.sharding import PartitionSpec as P

NB = 512
LX = 32
LY = 16
NZ = 192
CELLS = LX * LY
NPTS = NZ * CELLS
DEG = 4
DOM = 32
BAND = 16
TILE = NB // BAND
DEPTH = NZ // DOM
LANES = 128
ALL = ("band", "dom")

COEF = (
    -5369.0 / 1800.0,
    12.0 / 7.0,
    -15.0 / 56.0,
    10.0 / 189.0,
    -1.0 / 112.0,
    2.0 / 1925.0,
    -1.0 / 16632.0,
)
INV_SPACING2 = 4.0
CENTRE = 24.0
HALF_WIDTH = 20.0

HIGHEST = lax.Precision.HIGHEST
f32 = jnp.float32
bf16 = jnp.bfloat16


def split_constant(matrix):
    pieces = []
    rest = matrix.astype(np.float64)
    for _ in range(2):
        piece = rest.astype(np.float32).astype(bf16)
        pieces.append(piece)
        rest = rest - piece.astype(np.float64)
    return pieces


def plane_matrix():
    out = np.zeros((CELLS, CELLS))
    scale = -0.5 * INV_SPACING2 / HALF_WIDTH
    for y in range(LY):
        for x in range(LX):
            row = y * LX + x
            out[row, row] += scale * 3.0 * COEF[0] - CENTRE / HALF_WIDTH
            for k in range(1, 7):
                for step in (k, -k):
                    out[row, y * LX + (x + step) % LX] += scale * COEF[k]
                    out[row, (y + step) % LY * LX + x] += scale * COEF[k]
    return out


def layer_matrix():
    out = np.zeros((NZ, NZ))
    scale = -0.5 * INV_SPACING2 / HALF_WIDTH
    for k in range(1, 7):
        out += scale * COEF[k] * (np.eye(NZ, k=k) + np.eye(NZ, k=-k))
    return out


def split_value(value):
    high = value.astype(bf16)
    return high, (value - high.astype(f32)).astype(bf16)


def dot_split(left, right):
    def dot(a, b):
        return jnp.dot(a, b, preferred_element_type=f32)

    return (dot(left[0], right[1]) + dot(left[1], right[0])) + dot(left[0], right[0])


def pack_kernel(psi, potential, out):
    for layer in range(DEPTH):
        for quarter in range(4):
            lanes = slice(quarter * LANES, (quarter + 1) * LANES)
            row = layer * 8 + quarter
            out[pl.ds(row, TILE, stride=8 * DEPTH), :] = psi[layer, :, lanes]
            out[pl.ds(row + 4, TILE, stride=8 * DEPTH), :] = jnp.broadcast_to(
                potential[layer : layer + 1, lanes] * (1.0 / HALF_WIDTH), (TILE, LANES)
            )


def filter_kernel(rows, strip, m_layer, out, scratch, m_plane):
    for piece in range(2):
        for i in range(4):
            for j in range(4):
                at = (j - i) % 4 * LANES
                m_plane[piece, i * LANES : (i + 1) * LANES, j * LANES : (j + 1) * LANES] = strip[
                    piece, :, at : at + LANES
                ]
    start = jnp.concatenate([rows[pl.ds(q, NZ, stride=8), :] for q in range(4)], axis=1)
    potential = jnp.concatenate([rows[pl.ds(4 + q, NZ, stride=8), :] for q in range(4)], axis=1)
    plane = (m_plane[0], m_plane[1])
    layers = (m_layer[0], m_layer[1])

    def apply(values):
        pieces = split_value(values)
        return dot_split(pieces, plane) + dot_split(layers, pieces) + potential * values

    previous = start
    current = apply(start)
    for _ in range(1, DEG):
        previous, current = current, 2.0 * apply(current) - previous
    norm = jnp.sum(jnp.sum(current * current, axis=0, keepdims=True), axis=1, keepdims=True) * (
        1.0 / NPTS
    )
    for quarter in range(4):
        scratch[quarter * NZ : (quarter + 1) * NZ, :] = current[
            :, quarter * LANES : (quarter + 1) * LANES
        ]
    lane = lax.broadcasted_iota(jnp.int32, (DOM, LANES), 1)
    norms = jnp.broadcast_to(norm, (DOM, LANES))
    for piece in range(BAND):
        first = scratch[pl.ds((piece % 4) * NZ + piece // 4, DOM, stride=DEPTH), :]
        half = piece // 2
        second = scratch[pl.ds((half % 4) * NZ + 4 + half // 4, DOM, stride=DEPTH), :]
        if piece % 2:
            second = pltpu.roll(second, 64, 1)
        out[pl.ds(piece * 2 * DOM, DOM, stride=2), :] = first
        out[pl.ds(piece * 2 * DOM + 1, DOM, stride=2), :] = jnp.where(lane < 64, second, norms)


def points_of(rows):
    first = rows[pl.ds(0, NB, stride=2), :]
    second = rows[pl.ds(1, NB, stride=2), :]
    lane = lax.broadcasted_iota(jnp.int32, (NB, LANES), 1)
    return first, jnp.where(lane < 64, second, 0.0), second


def dot_nt(a, b):
    return lax.dot_general(
        a, b, (((1,), (1,)), ((), ())), precision=HIGHEST, preferred_element_type=f32
    )


def dot_nn(a, b):
    return jnp.dot(a, b, precision=HIGHEST, preferred_element_type=f32)


def gram_kernel(rows, out):
    first, second, _ = points_of(rows)
    points = jnp.concatenate([first, second], axis=1)
    low, high = points[:256], points[256:]
    row = lax.broadcasted_iota(jnp.int32, (256, 256), 0)
    col = lax.broadcasted_iota(jnp.int32, (256, 256), 1)
    folded = jnp.where(col <= row, dot_nt(low, low), dot_nt(high, high))
    below = dot_nt(high, low)
    out[0:256, :] = folded[:, :LANES]
    out[256:512, :] = folded[:, LANES:]
    out[512:768, :] = below[:, :LANES]
    out[768:1024, :] = below[:, LANES:]


def sum_kernel(parts, out):
    total = jnp.sum(parts[...].reshape(8, 16, 8, LANES), axis=0)
    total = jnp.sum(total, axis=0)
    total = total + pltpu.roll(total, 4, 0)
    total = (total + pltpu.roll(total, 2, 0)) * (1.0 / NPTS)
    out[...] = jnp.broadcast_to(total[None], (NB // 4, 8, LANES)).reshape(2 * NB, LANES)


def invert_block(m, ones):
    full = (8, LANES)
    sub = lax.broadcasted_iota(jnp.int32, full, 0)
    lane = lax.broadcasted_iota(jnp.int32, full, 1)

    def row(value, u):
        return jnp.broadcast_to(value[u : u + 1, :], full)

    def column(value, at):
        return jnp.broadcast_to(value[:, at : at + 1], full)

    for panel in range(16):
        base = 8 * panel
        inside = (lane >= base) & (lane < base + 8)
        v = m[base : base + 8, :]
        a = [column(v, base + t) * ones for t in range(8)]
        v = jnp.where(inside, jnp.where(lane - base == sub, 1.0, 0.0), v)
        v_rows = [row(v, u) for u in range(8)]
        lower = [jnp.zeros(full, f32) for _ in range(7)]
        scale = jnp.zeros(full, f32)
        for k in range(8):
            here = sub == k
            pivots = [row(a[k], j) for j in range(8)]
            root = lax.rsqrt(pivots[k])
            inverse = root * root
            for t in range(k):
                lower[t] = jnp.where(here, a[t], lower[t])
            scale = jnp.where(here, root, scale)
            swept = jnp.where(here, -inverse, a[k] * inverse)
            for j in range(8):
                if j != k:
                    a[j] = jnp.where(here, 0.0, a[j]) - swept * pivots[j]
            a[k] = swept
        done = v
        for t in range(7):
            done = done - lower[t] * v_rows[t]
        m[base : base + 8, :] = jnp.where(lane < base + 8, done * scale, 0.0)
        y = [a[u] * v_rows[u] for u in range(8)]
        y = ((y[0] + y[1]) + (y[2] + y[3])) + ((y[4] + y[5]) + (y[6] + y[7]))
        y_rows = [row(y, u) for u in range(8)]
        for q in range(panel + 1, 16):
            d = m[8 * q : 8 * q + 8, :]
            u = [column(d, base + t) * y_rows[t] for t in range(8)]
            u = ((u[0] + u[1]) + (u[2] + u[3])) + ((u[4] + u[5]) + (u[6] + u[7]))
            m[8 * q : 8 * q + 8, :] = jnp.where(inside, 0.0, d) + u


def solve_kernel(gram, rows, out, s_ref, x_ref, block, ones_ref):
    first, second, raw = points_of(rows)
    x_ref[:, :LANES] = first
    x_ref[:, LANES:] = second
    ones_ref[...] = jnp.ones((8, LANES), f32)
    folded = jnp.concatenate([gram[0:256, :], gram[256:512, :]], axis=1)
    flipped = folded.T
    row = lax.broadcasted_iota(jnp.int32, (256, 256), 0)
    col = lax.broadcasted_iota(jnp.int32, (256, 256), 1)
    low = jnp.where(col <= row, folded, flipped)
    norms = jnp.broadcast_to(raw[256:, LANES - 1 : LANES], (256, 256))
    high = jnp.where(col == row, norms, jnp.where(col > row, folded, flipped))
    s_ref[0, :256, :] = low[:, :LANES]
    s_ref[1, :256, :] = low[:, LANES:]
    s_ref[0, 256:, :] = gram[512:768, :]
    s_ref[1, 256:, :] = gram[768:1024, :]
    s_ref[2, 256:, :] = high[:, :LANES]
    s_ref[3, 256:, :] = high[:, LANES:]

    def step(j, carry):
        at = pl.ds(pl.multiple_of(j * LANES, LANES), LANES)
        block[...] = s_ref[j, at, :]
        invert_block(block, ones_ref[...])
        inverse = block[...]
        x_ref[at, :] = dot_nn(inverse, x_ref[at, :])
        for now in range(3):

            @pl.when(j == now)
            def _():
                here = slice(now * LANES, (now + 1) * LANES)
                rest = slice((now + 1) * LANES, NB)
                panel = dot_nt(s_ref[now, rest, :], inverse)
                x_ref[rest, :] = x_ref[rest, :] - dot_nn(panel, x_ref[here, :])
                for k in range(now + 1, 4):
                    skip = (k - now - 1) * LANES
                    s_ref[k, k * LANES :, :] = s_ref[k, k * LANES :, :] - dot_nt(
                        panel[skip:], panel[skip : skip + LANES]
                    )

        return carry

    lax.fori_loop(0, 4, step, 0)
    for tile in range(BAND):
        at = tile * TILE
        out[tile * 48 : tile * 48 + 32, :] = x_ref[at : at + TILE, :LANES]
        out[tile * 48 + 32 : tile * 48 + 48, :] = x_ref[at : at + 16, LANES:] + pltpu.roll(
            x_ref[at + 16 : at + 32, LANES:], 64, 1
        )


def unpack_kernel(rows, out):
    for piece in range(BAND):
        quarter = piece % 4
        out[piece // 4, :, quarter * LANES : (quarter + 1) * LANES] = rows[
            piece * 48 : piece * 48 + 32, :
        ]
    lower = lax.broadcasted_iota(jnp.int32, (16, LANES), 1) < 64
    for half in range(8):
        lanes = slice((half % 4) * LANES, (half % 4 + 1) * LANES)
        even = rows[2 * half * 48 + 32 : 2 * half * 48 + 48, :]
        odd = rows[(2 * half + 1) * 48 + 32 : (2 * half + 1) * 48 + 48, :]
        out[4 + half // 4, 0:16, lanes] = jnp.where(lower, even, pltpu.roll(odd, 64, 1))
        out[4 + half // 4, 16:32, lanes] = jnp.where(lower, pltpu.roll(even, 64, 1), odd)


def whole():
    return pl.BlockSpec(memory_space=pltpu.VMEM)


def call(kernel, name, shape, specs, scratch=()):
    return pl.pallas_call(
        kernel,
        name=name,
        out_shape=jax.ShapeDtypeStruct(shape, f32),
        in_specs=specs,
        out_specs=whole(),
        scratch_shapes=list(scratch),
        compiler_params=pltpu.CompilerParams(vmem_limit_bytes=48 << 20),
    )


def do_pack(psi, potential):
    return call(pack_kernel, "pack", (TILE * 8 * DEPTH, LANES), [whole()] * 2)(psi, potential)


def do_filter(rows):
    strip = np.stack(split_constant(plane_matrix()[:LANES]))
    layers = np.stack(split_constant(layer_matrix()))
    return call(
        filter_kernel,
        "filter",
        (2 * NB, LANES),
        [whole()] * 3,
        [pltpu.VMEM((4 * NZ, LANES), f32), pltpu.VMEM((2, CELLS, CELLS), bf16)],
    )(rows, jnp.asarray(strip), jnp.asarray(layers))


def do_gram(rows):
    return call(gram_kernel, "gram", (2 * NB, LANES), [whole()])(rows)


def do_sum(parts):
    return call(sum_kernel, "sum", (2 * NB, LANES), [whole()])(parts)


def do_solve(gram, rows):
    return call(
        solve_kernel,
        "solve",
        (BAND * 48, LANES),
        [whole(), whole()],
        [
            pltpu.VMEM((4, NB, LANES), f32),
            pltpu.VMEM((NB, 2 * LANES), f32),
            pltpu.VMEM((LANES, LANES), f32),
            pltpu.VMEM((8, LANES), f32),
        ],
    )(gram, rows)


def do_unpack(rows):
    return call(unpack_kernel, "unpack", (DEPTH, TILE, CELLS), [whole()])(rows)


def exchange(rows, axis, parts):
    shaped = rows.reshape(parts, rows.shape[0] // parts, LANES)
    return lax.all_to_all(shaped, axis, 0, 0).reshape(rows.shape)


def shards(psi, potential):
    bands = exchange(do_pack(jnp.transpose(psi, (1, 0, 2)), potential), "dom", DOM)
    points = exchange(do_filter(bands), ALL, NB)
    parts = exchange(do_gram(points), ALL, NB)
    gram = exchange(do_sum(parts), ALL, NB)
    result = exchange(do_solve(gram, points), "band", BAND)
    return jnp.transpose(do_unpack(result), (1, 0, 2))


def solution(mesh):
    placed = (P("band", "dom", None), P("dom", None))
    return jax.shard_map(
        shards, mesh=mesh, in_specs=placed, out_specs=P("band", "dom", None), check_vma=False
    )
```

```python
import jax
import jax.numpy as jnp
import numpy as np
from jax import lax
from jax.experimental import pallas as pl
from jax.experimental.pallas import tpu as pltpu
from jax.sharding import Mesh, PartitionSpec as P

NB = 512
LX = 32
LY = 16
NZ = 192
CELLS = LX * LY
NPTS = NZ * CELLS
DEG = 4
DOM = 32
BAND = 16
TILE = NB // BAND
DEPTH = NZ // DOM
LANES = 128
SIDES = (8, 2, 2, 8, 2)
NAMES = ("y", "xh", "core", "z", "xl")
LAYERS = ("y", "xh", "core")
BANDS = ("z", "xl")
ALL = BANDS + LAYERS
PLANE = ("y", "xh", "xl")
IN_PLANE = 32

COEF = (
    -5369.0 / 1800.0,
    12.0 / 7.0,
    -15.0 / 56.0,
    10.0 / 189.0,
    -1.0 / 112.0,
    2.0 / 1925.0,
    -1.0 / 16632.0,
)
INV_SPACING2 = 4.0
CENTRE = 24.0
HALF_WIDTH = 20.0

HIGHEST = lax.Precision.HIGHEST
f32 = jnp.float32
bf16 = jnp.bfloat16


def split_constant(matrix):
    pieces = []
    rest = matrix.astype(np.float64)
    for _ in range(2):
        piece = rest.astype(np.float32).astype(bf16)
        pieces.append(piece)
        rest = rest - piece.astype(np.float64)
    return pieces


def plane_matrix():
    out = np.zeros((CELLS, CELLS))
    scale = -0.5 * INV_SPACING2 / HALF_WIDTH
    for y in range(LY):
        for x in range(LX):
            row = y * LX + x
            out[row, row] += scale * 3.0 * COEF[0] - CENTRE / HALF_WIDTH
            for k in range(1, 7):
                for step in (k, -k):
                    out[row, y * LX + (x + step) % LX] += scale * COEF[k]
                    out[row, (y + step) % LY * LX + x] += scale * COEF[k]
    return out


def layer_matrix():
    out = np.zeros((NZ, NZ))
    scale = -0.5 * INV_SPACING2 / HALF_WIDTH
    for k in range(1, 7):
        out += scale * COEF[k] * (np.eye(NZ, k=k) + np.eye(NZ, k=-k))
    return out


def split_value(value):
    high = value.astype(bf16)
    return high, (value - high.astype(f32)).astype(bf16)


def dot_split(left, right):
    def dot(a, b):
        return jnp.dot(a, b, preferred_element_type=f32)

    return (dot(left[0], right[1]) + dot(left[1], right[0])) + dot(left[0], right[0])


def pack_kernel(psi, potential, out):
    for layer in range(DEPTH):
        for quarter in range(4):
            lanes = slice(quarter * LANES, (quarter + 1) * LANES)
            row = layer * 8 + quarter
            out[pl.ds(row, TILE, stride=8 * DEPTH), :] = psi[layer, :, lanes]
            out[pl.ds(row + 4, TILE, stride=8 * DEPTH), :] = jnp.broadcast_to(
                potential[layer : layer + 1, lanes] * (1.0 / HALF_WIDTH), (TILE, LANES)
            )


def filter_kernel(rows, strip, m_layer, out, scratch, m_plane):
    for piece in range(2):
        for i in range(4):
            for j in range(4):
                at = (j - i) % 4 * LANES
                m_plane[piece, i * LANES : (i + 1) * LANES, j * LANES : (j + 1) * LANES] = strip[
                    piece, :, at : at + LANES
                ]
    start = jnp.concatenate([rows[pl.ds(q, NZ, stride=8), :] for q in range(4)], axis=1)
    potential = jnp.concatenate([rows[pl.ds(4 + q, NZ, stride=8), :] for q in range(4)], axis=1)
    plane = (m_plane[0], m_plane[1])
    layers = (m_layer[0], m_layer[1])

    def apply(values):
        pieces = split_value(values)
        return dot_split(pieces, plane) + dot_split(layers, pieces) + potential * values

    previous = start
    current = apply(start)
    for _ in range(1, DEG):
        previous, current = current, 2.0 * apply(current) - previous
    norm = jnp.sum(jnp.sum(current * current, axis=0, keepdims=True), axis=1, keepdims=True) * (
        1.0 / NPTS
    )
    for quarter in range(4):
        scratch[quarter * NZ : (quarter + 1) * NZ, :] = current[
            :, quarter * LANES : (quarter + 1) * LANES
        ]
    lane = lax.broadcasted_iota(jnp.int32, (DOM, LANES), 1)
    norms = jnp.broadcast_to(norm, (DOM, LANES))
    for piece in range(BAND):
        first = scratch[pl.ds((piece % 4) * NZ + piece // 4, DOM, stride=DEPTH), :]
        half = piece // 2
        second = scratch[pl.ds((half % 4) * NZ + 4 + half // 4, DOM, stride=DEPTH), :]
        if piece % 2:
            second = pltpu.roll(second, 64, 1)
        out[pl.ds(piece * 2 * DOM, DOM, stride=2), :] = first
        out[pl.ds(piece * 2 * DOM + 1, DOM, stride=2), :] = jnp.where(lane < 64, second, norms)


def points_of(rows):
    first = rows[pl.ds(0, NB, stride=2), :]
    second = rows[pl.ds(1, NB, stride=2), :]
    lane = lax.broadcasted_iota(jnp.int32, (NB, LANES), 1)
    return first, jnp.where(lane < 64, second, 0.0), second


def dot_nt(a, b):
    return lax.dot_general(
        a, b, (((1,), (1,)), ((), ())), precision=HIGHEST, preferred_element_type=f32
    )


def dot_nn(a, b):
    return jnp.dot(a, b, precision=HIGHEST, preferred_element_type=f32)


def gram_kernel(core, rows, keep, send):
    first, second, _ = points_of(rows)
    points = jnp.concatenate([first, second], axis=1)
    low, high = points[:256], points[256:]
    row = lax.broadcasted_iota(jnp.int32, (256, 256), 0)
    col = lax.broadcasted_iota(jnp.int32, (256, 256), 1)
    folded = jnp.where(col <= row, dot_nt(low, low), dot_nt(high, high))
    below = dot_nt(high, low)
    first = core[0] == 0
    for half in range(2):
        lanes = slice(half * LANES, (half + 1) * LANES)
        at = slice(half * 256, (half + 1) * 256)
        keep[at, :] = jnp.where(first, folded[:, lanes], below[:, lanes])
        send[at, :] = jnp.where(first, below[:, lanes], folded[:, lanes])


def sum_kernel(scale):
    def kernel(parts, out):
        total = jnp.sum(parts[...], axis=0) * scale
        out[...] = jnp.broadcast_to(total[None], out.shape)

    return kernel


def invert_block(m, ones):
    full = (8, LANES)
    sub = lax.broadcasted_iota(jnp.int32, full, 0)
    lane = lax.broadcasted_iota(jnp.int32, full, 1)

    def row(value, u):
        return jnp.broadcast_to(value[u : u + 1, :], full)

    def column(value, at):
        return jnp.broadcast_to(value[:, at : at + 1], full)

    for panel in range(16):
        base = 8 * panel
        inside = (lane >= base) & (lane < base + 8)
        v = m[base : base + 8, :]
        a = [column(v, base + t) * ones for t in range(8)]
        v = jnp.where(inside, jnp.where(lane - base == sub, 1.0, 0.0), v)
        v_rows = [row(v, u) for u in range(8)]
        lower = [jnp.zeros(full, f32) for _ in range(7)]
        scale = jnp.zeros(full, f32)
        for k in range(8):
            here = sub == k
            pivots = [row(a[k], j) for j in range(8)]
            root = lax.rsqrt(pivots[k])
            inverse = root * root
            for t in range(k):
                lower[t] = jnp.where(here, a[t], lower[t])
            scale = jnp.where(here, root, scale)
            swept = jnp.where(here, -inverse, a[k] * inverse)
            for j in range(8):
                if j != k:
                    a[j] = jnp.where(here, 0.0, a[j]) - swept * pivots[j]
            a[k] = swept
        done = v
        for t in range(7):
            done = done - lower[t] * v_rows[t]
        m[base : base + 8, :] = jnp.where(lane < base + 8, done * scale, 0.0)
        y = [a[u] * v_rows[u] for u in range(8)]
        y = ((y[0] + y[1]) + (y[2] + y[3])) + ((y[4] + y[5]) + (y[6] + y[7]))
        y_rows = [row(y, u) for u in range(8)]
        for q in range(panel + 1, 16):
            d = m[8 * q : 8 * q + 8, :]
            u = [column(d, base + t) * y_rows[t] for t in range(8)]
            u = ((u[0] + u[1]) + (u[2] + u[3])) + ((u[4] + u[5]) + (u[6] + u[7]))
            m[8 * q : 8 * q + 8, :] = jnp.where(inside, 0.0, d) + u


def solve_kernel(core, mine, other, rows, out, s_ref, x_ref, block, ones_ref):
    first, second, raw = points_of(rows)
    x_ref[:, :LANES] = first
    x_ref[:, LANES:] = second
    ones_ref[...] = jnp.ones((8, LANES), f32)
    swap = core[0] == 0
    folded = jnp.where(swap, mine[...], other[...])
    folded = jnp.concatenate([folded[:256], folded[256:]], axis=1)
    flipped = folded.T
    row = lax.broadcasted_iota(jnp.int32, (256, 256), 0)
    col = lax.broadcasted_iota(jnp.int32, (256, 256), 1)
    low = jnp.where(col <= row, folded, flipped)
    norms = jnp.broadcast_to(raw[256:, LANES - 1 : LANES], (256, 256))
    high = jnp.where(col == row, norms, jnp.where(col > row, folded, flipped))
    s_ref[0, :256, :] = low[:, :LANES]
    s_ref[1, :256, :] = low[:, LANES:]
    s_ref[0, 256:, :] = jnp.where(swap, other[:256, :], mine[:256, :])
    s_ref[1, 256:, :] = jnp.where(swap, other[256:, :], mine[256:, :])
    s_ref[2, 256:, :] = high[:, :LANES]
    s_ref[3, 256:, :] = high[:, LANES:]

    def step(j, carry):
        at = pl.ds(pl.multiple_of(j * LANES, LANES), LANES)
        block[...] = s_ref[j, at, :]
        invert_block(block, ones_ref[...])
        inverse = block[...]
        x_ref[at, :] = dot_nn(inverse, x_ref[at, :])
        for now in range(3):

            @pl.when(j == now)
            def _():
                here = slice(now * LANES, (now + 1) * LANES)
                rest = slice((now + 1) * LANES, NB)
                panel = dot_nt(s_ref[now, rest, :], inverse)
                x_ref[rest, :] = x_ref[rest, :] - dot_nn(panel, x_ref[here, :])
                for k in range(now + 1, 4):
                    skip = (k - now - 1) * LANES
                    s_ref[k, k * LANES :, :] = s_ref[k, k * LANES :, :] - dot_nt(
                        panel[skip:], panel[skip : skip + LANES]
                    )

        return carry

    lax.fori_loop(0, 4, step, 0)
    for tile in range(BAND):
        at = tile * TILE
        out[tile * 48 : tile * 48 + 32, :] = x_ref[at : at + TILE, :LANES]
        out[tile * 48 + 32 : tile * 48 + 48, :] = x_ref[at : at + 16, LANES:] + pltpu.roll(
            x_ref[at + 16 : at + 32, LANES:], 64, 1
        )


def unpack_kernel(rows, out):
    for piece in range(BAND):
        quarter = piece % 4
        out[piece // 4, :, quarter * LANES : (quarter + 1) * LANES] = rows[
            piece * 48 : piece * 48 + 32, :
        ]
    lower = lax.broadcasted_iota(jnp.int32, (16, LANES), 1) < 64
    for half in range(8):
        lanes = slice((half % 4) * LANES, (half % 4 + 1) * LANES)
        even = rows[2 * half * 48 + 32 : 2 * half * 48 + 48, :]
        odd = rows[(2 * half + 1) * 48 + 32 : (2 * half + 1) * 48 + 48, :]
        out[4 + half // 4, 0:16, lanes] = jnp.where(lower, even, pltpu.roll(odd, 64, 1))
        out[4 + half // 4, 16:32, lanes] = jnp.where(lower, pltpu.roll(even, 64, 1), odd)


def whole():
    return pl.BlockSpec(memory_space=pltpu.VMEM)


def scalar():
    return pl.BlockSpec(memory_space=pltpu.SMEM)


def call(kernel, name, shape, specs, scratch=()):
    return pl.pallas_call(
        kernel,
        name=name,
        out_shape=jax.ShapeDtypeStruct(shape, f32),
        in_specs=specs,
        out_specs=whole(),
        scratch_shapes=list(scratch),
        compiler_params=pltpu.CompilerParams(vmem_limit_bytes=48 << 20),
    )


def do_pack(psi, potential):
    return call(pack_kernel, "pack", (TILE * 8 * DEPTH, LANES), [whole()] * 2)(psi, potential)


def do_filter(rows):
    strip = np.stack(split_constant(plane_matrix()[:LANES]))
    layers = np.stack(split_constant(layer_matrix()))
    return call(
        filter_kernel,
        "filter",
        (2 * NB, LANES),
        [whole()] * 3,
        [pltpu.VMEM((4 * NZ, LANES), f32), pltpu.VMEM((2, CELLS, CELLS), bf16)],
    )(rows, jnp.asarray(strip), jnp.asarray(layers))


def do_gram(core, rows):
    half = jax.ShapeDtypeStruct((NB, LANES), f32)
    return pl.pallas_call(
        gram_kernel,
        name="gram",
        out_shape=(half, half),
        in_specs=[scalar(), whole()],
        out_specs=(whole(), whole()),
        compiler_params=pltpu.CompilerParams(vmem_limit_bytes=48 << 20),
    )(core, rows)


def do_sum(parts, copies, scale):
    return call(sum_kernel(scale), "sum", (copies,) + parts.shape[1:], [whole()])(parts)


def do_solve(core, mine, other, rows):
    return call(
        solve_kernel,
        "solve",
        (BAND * 48, LANES),
        [scalar(), whole(), whole(), whole()],
        [
            pltpu.VMEM((4, NB, LANES), f32),
            pltpu.VMEM((NB, 2 * LANES), f32),
            pltpu.VMEM((LANES, LANES), f32),
            pltpu.VMEM((8, LANES), f32),
        ],
    )(core, mine, other, rows)


def do_unpack(rows):
    return call(unpack_kernel, "unpack", (DEPTH, TILE, CELLS), [whole()])(rows)


def exchange(rows, axis, parts):
    shaped = rows.reshape(parts, rows.shape[0] // parts, LANES)
    return lax.all_to_all(shaped, axis, 0, 0).reshape(rows.shape)


def swap_cores(value):
    return lax.ppermute(value, "core", [(0, 1), (1, 0)])


def gram_sum(keep, send):
    depth = SIDES[3]
    half = (keep + swap_cores(send)).reshape(IN_PLANE, NB // IN_PLANE, LANES)
    half = do_sum(lax.all_to_all(half, PLANE, 0, 0), depth, 1.0)
    half = do_sum(lax.all_to_all(half, "z", 0, 0), IN_PLANE, 1.0 / NPTS)
    return lax.all_to_all(half, PLANE, 0, 0).reshape(NB, LANES)


def shards(psi, potential):
    core = lax.axis_index("core").astype(jnp.int32).reshape(1)
    psi, core = lax.optimization_barrier((psi, core))
    bands = exchange(do_pack(jnp.transpose(psi, (1, 0, 2)), potential), LAYERS, DOM)
    points = exchange(do_filter(bands), ALL, NB)
    gram = gram_sum(*do_gram(core, points))
    result = exchange(do_solve(core, gram, swap_cores(gram), points), BANDS, BAND)
    return jnp.transpose(do_unpack(result), (1, 0, 2))


def solution(mesh):
    split = Mesh(np.asarray(mesh.devices).reshape(SIDES), NAMES)
    bands = P(BANDS, LAYERS, None)
    return jax.shard_map(
        shards, mesh=split, in_specs=(bands, P(LAYERS, None)), out_specs=bands, check_vma=False
    )
```

```python
import jax
import jax.numpy as jnp
import numpy as np
from jax import lax
from jax.experimental import pallas as pl
from jax.experimental.pallas import tpu as pltpu
from jax.sharding import Mesh, PartitionSpec as P

NB = 512
LX = 32
LY = 16
NZ = 192
CELLS = LX * LY
NPTS = NZ * CELLS
DEG = 4
DOM = 32
BAND = 16
TILE = NB // BAND
DEPTH = NZ // DOM
LANES = 128
SIDES = (8, 2, 2, 8, 2)
NAMES = ("y", "xh", "core", "z", "xl")
LAYERS = ("y", "xh", "core")
BANDS = ("z", "xl")
ALL = BANDS + LAYERS
PLANE = ("y", "xh", "xl")
IN_PLANE = 32

COEF = (
    -5369.0 / 1800.0,
    12.0 / 7.0,
    -15.0 / 56.0,
    10.0 / 189.0,
    -1.0 / 112.0,
    2.0 / 1925.0,
    -1.0 / 16632.0,
)
INV_SPACING2 = 4.0
CENTRE = 24.0
HALF_WIDTH = 20.0

HIGHEST = lax.Precision.HIGHEST
f32 = jnp.float32
bf16 = jnp.bfloat16


def split_constant(matrix):
    pieces = []
    rest = matrix.astype(np.float64)
    for _ in range(2):
        piece = rest.astype(np.float32).astype(bf16)
        pieces.append(piece)
        rest = rest - piece.astype(np.float64)
    return pieces


def plane_matrix():
    out = np.zeros((CELLS, CELLS))
    scale = -0.5 * INV_SPACING2 / HALF_WIDTH
    for y in range(LY):
        for x in range(LX):
            row = y * LX + x
            out[row, row] += scale * 3.0 * COEF[0] - CENTRE / HALF_WIDTH
            for k in range(1, 7):
                for step in (k, -k):
                    out[row, y * LX + (x + step) % LX] += scale * COEF[k]
                    out[row, (y + step) % LY * LX + x] += scale * COEF[k]
    return out


def layer_matrix():
    out = np.zeros((NZ, NZ))
    scale = -0.5 * INV_SPACING2 / HALF_WIDTH
    for k in range(1, 7):
        out += scale * COEF[k] * (np.eye(NZ, k=k) + np.eye(NZ, k=-k))
    return out


def split_value(value):
    high = value.astype(bf16)
    return high, (value - high.astype(f32)).astype(bf16)


def dot_split(left, right):
    def dot(a, b):
        return jnp.dot(a, b, preferred_element_type=f32)

    return (dot(left[0], right[1]) + dot(left[1], right[0])) + dot(left[0], right[0])


def pack_kernel(psi, potential, out):
    for layer in range(DEPTH):
        for quarter in range(4):
            lanes = slice(quarter * LANES, (quarter + 1) * LANES)
            row = layer * 8 + quarter
            out[pl.ds(row, TILE, stride=8 * DEPTH), :] = psi[layer, :, lanes]
            out[pl.ds(row + 4, TILE, stride=8 * DEPTH), :] = jnp.broadcast_to(
                potential[layer : layer + 1, lanes] * (1.0 / HALF_WIDTH), (TILE, LANES)
            )


def filter_kernel(rows, strip, m_layer, out, scratch, m_plane):
    for piece in range(2):
        for i in range(4):
            for j in range(4):
                at = (j - i) % 4 * LANES
                m_plane[piece, i * LANES : (i + 1) * LANES, j * LANES : (j + 1) * LANES] = strip[
                    piece, :, at : at + LANES
                ]
    start = jnp.concatenate([rows[pl.ds(q, NZ, stride=8), :] for q in range(4)], axis=1)
    potential = jnp.concatenate([rows[pl.ds(4 + q, NZ, stride=8), :] for q in range(4)], axis=1)
    plane = (m_plane[0], m_plane[1])
    layers = (m_layer[0], m_layer[1])

    def apply(values):
        pieces = split_value(values)
        return dot_split(pieces, plane) + dot_split(layers, pieces) + potential * values

    previous = start
    current = apply(start)
    for _ in range(1, DEG):
        previous, current = current, 2.0 * apply(current) - previous
    norm = jnp.sum(jnp.sum(current * current, axis=0, keepdims=True), axis=1, keepdims=True) * (
        1.0 / NPTS
    )
    for quarter in range(4):
        scratch[quarter * NZ : (quarter + 1) * NZ, :] = current[
            :, quarter * LANES : (quarter + 1) * LANES
        ]
    lane = lax.broadcasted_iota(jnp.int32, (DOM, LANES), 1)
    norms = jnp.broadcast_to(norm, (DOM, LANES))
    for piece in range(BAND):
        first = scratch[pl.ds((piece % 4) * NZ + piece // 4, DOM, stride=DEPTH), :]
        half = piece // 2
        second = scratch[pl.ds((half % 4) * NZ + 4 + half // 4, DOM, stride=DEPTH), :]
        if piece % 2:
            second = pltpu.roll(second, 64, 1)
        out[pl.ds(piece * 2 * DOM, DOM, stride=2), :] = first
        out[pl.ds(piece * 2 * DOM + 1, DOM, stride=2), :] = jnp.where(lane < 64, second, norms)


def points_of(rows):
    first = rows[pl.ds(0, NB, stride=2), :]
    second = rows[pl.ds(1, NB, stride=2), :]
    lane = lax.broadcasted_iota(jnp.int32, (NB, LANES), 1)
    return first, jnp.where(lane < 64, second, 0.0), second


def dot_nt(a, b):
    return lax.dot_general(
        a, b, (((1,), (1,)), ((), ())), precision=HIGHEST, preferred_element_type=f32
    )


def gram_kernel(core, rows, keep, send):
    first, second, _ = points_of(rows)
    points = jnp.concatenate([first, second], axis=1)
    low, high = points[:256], points[256:]
    row = lax.broadcasted_iota(jnp.int32, (256, 256), 0)
    col = lax.broadcasted_iota(jnp.int32, (256, 256), 1)
    folded = jnp.where(col <= row, dot_nt(low, low), dot_nt(high, high))
    below = dot_nt(high, low)
    first = core[0] == 0
    for half in range(2):
        lanes = slice(half * LANES, (half + 1) * LANES)
        at = slice(half * 256, (half + 1) * 256)
        keep[at, :] = jnp.where(first, folded[:, lanes], below[:, lanes])
        send[at, :] = jnp.where(first, below[:, lanes], folded[:, lanes])


def sum_kernel(scale):
    def kernel(parts, out):
        total = jnp.sum(parts[...], axis=0) * scale
        out[...] = jnp.broadcast_to(total[None], out.shape)

    return kernel


def invert_block(m, ones, work):
    full = (8, LANES)
    sub = lax.broadcasted_iota(jnp.int32, full, 0)
    lane = lax.broadcasted_iota(jnp.int32, full, 1)

    def row(value, u):
        return jnp.broadcast_to(value[u : u + 1, :], full)

    def column(value, at):
        return jnp.broadcast_to(value[:, at : at + 1], full)

    def total(terms):
        return ((terms[0] + terms[1]) + (terms[2] + terms[3])) + (
            (terms[4] + terms[5]) + (terms[6] + terms[7])
        )

    v = m[0:8, :]
    for panel in range(16):
        base = 8 * panel
        inside = (lane >= base) & (lane < base + 8)
        a = [column(v, base + t) * ones for t in range(8)]
        v = jnp.where(inside, jnp.where(lane - base == sub, 1.0, 0.0), v)
        v_rows = [row(v, u) for u in range(8)]
        lower = [jnp.zeros(full, f32) for _ in range(7)]
        scale = jnp.zeros(full, f32)
        pivots = [row(a[0], j) for j in range(8)]
        for k in range(8):
            here = sub == k
            ahead = [row(a[k], j) for j in range(k)] + pivots[k:]
            root = lax.rsqrt(ahead[k])
            inverse = root * root
            if k < 7:
                pivots = [None] * (k + 1) + [
                    row(a[k + 1], j) - (ahead[k + 1] * ahead[j]) * inverse for j in range(k + 1, 8)
                ]
            for t in range(k):
                lower[t] = jnp.where(here, a[t], lower[t])
            scale = jnp.where(here, root, scale)
            swept = jnp.where(here, -inverse, a[k] * inverse)
            for j in range(8):
                if j != k:
                    a[j] = jnp.where(here, 0.0, a[j]) - swept * ahead[j]
            a[k] = swept
        y = total([a[u] * v_rows[u] for u in range(8)])
        y_rows = [row(y, u) for u in range(8)]
        done = v
        for t in range(7):
            done = done - lower[t] * v_rows[t]
        m[base : base + 8, :] = jnp.where(lane < base + 8, done * scale, 0.0)
        for q in range(panel + 1, 16):
            d = m[8 * q : 8 * q + 8, :]
            d = jnp.where(inside, 0.0, d) + total([column(d, base + t) * y_rows[t] for t in range(8)])
            if q == panel + 1:
                v = d
            else:
                m[8 * q : 8 * q + 8, :] = d
        for _ in range(-(-len(work) // (16 - panel))):
            work.pop(0)()


def solve_kernel(core, mine, other, rows, out, s_ref, x_ref, blocks, panels, inverses, ones_ref):
    first, second, raw = points_of(rows)
    x_ref[:, :LANES] = first
    x_ref[:, LANES:] = second
    ones_ref[...] = jnp.ones((8, LANES), f32)
    swap = core[0] == 0
    folded = jnp.where(swap, mine[...], other[...])
    folded = jnp.concatenate([folded[:256], folded[256:]], axis=1)
    flipped = folded.T
    row = lax.broadcasted_iota(jnp.int32, (256, 256), 0)
    col = lax.broadcasted_iota(jnp.int32, (256, 256), 1)
    low = jnp.where(col <= row, folded, flipped)
    norms = jnp.broadcast_to(raw[256:, LANES - 1 : LANES], (256, 256))
    high = jnp.where(col == row, norms, jnp.where(col > row, folded, flipped))
    s_ref[0, :256, :] = low[:, :LANES]
    s_ref[1, :256, :] = low[:, LANES:]
    s_ref[0, 256:, :] = jnp.where(swap, other[:256, :], mine[:256, :])
    s_ref[1, 256:, :] = jnp.where(swap, other[256:, :], mine[256:, :])
    s_ref[2, 256:, :] = high[:, :LANES]
    s_ref[3, 256:, :] = high[:, LANES:]

    def at(i):
        return slice(i * LANES, (i + 1) * LANES)

    def split_dot(left, right, dims):
        def dot(a, b):
            return lax.dot_general(a, b, (dims, ((), ())), preferred_element_type=f32)

        return (dot(left[0], right[1]) + dot(left[1], right[0])) + dot(left[0], right[0])

    nt, nn = ((1,), (1,)), ((1,), (0,))

    def pieces(ref, i):
        return ref[i, 0], ref[i, 1]

    def put(ref, i, value):
        ref[i, 0], ref[i, 1] = split_value(value)

    def form_panel(j, i):
        put(panels, i, split_dot(split_value(s_ref[j, at(i), :]), pieces(inverses, j), nt))

    def update_s(k, i):
        s_ref[k, at(i), :] = s_ref[k, at(i), :] - split_dot(
            pieces(panels, i), pieces(panels, k), nt
        )

    def solve_x(j):
        x_ref[at(j), :] = split_dot(pieces(inverses, j), split_value(x_ref[at(j), :]), nn)

    def update_x(j, i):
        x_ref[at(i), :] = x_ref[at(i), :] - split_dot(
            pieces(panels, i), split_value(x_ref[at(j), :]), nn
        )

    ones = ones_ref[...]
    work = []
    blocks[0] = s_ref[0, at(0), :]
    for j in range(4):
        invert_block(blocks.at[j], ones, work)
        put(inverses, j, blocks[j])
        work = []
        if j < 3:
            form_panel(j, j + 1)
            blocks[j + 1] = s_ref[j + 1, at(j + 1), :] - split_dot(
                pieces(panels, j + 1), pieces(panels, j + 1), nt
            )
            for i in range(j + 2, 4):
                work.append(lambda j=j, i=i: form_panel(j, i))
                work.append(lambda k=j + 1, i=i: update_s(k, i))
            for k in range(j + 2, 4):
                for i in range(k, 4):
                    work.append(lambda k=k, i=i: update_s(k, i))
        work.append(lambda j=j: solve_x(j))
        for i in range(j + 1, 4):
            work.append(lambda j=j, i=i: update_x(j, i))
    for call_ in work:
        call_()
    for tile in range(BAND):
        at_ = tile * TILE
        out[tile * 48 : tile * 48 + 32, :] = x_ref[at_ : at_ + TILE, :LANES]
        out[tile * 48 + 32 : tile * 48 + 48, :] = x_ref[at_ : at_ + 16, LANES:] + pltpu.roll(
            x_ref[at_ + 16 : at_ + 32, LANES:], 64, 1
        )


def unpack_kernel(rows, out):
    for piece in range(BAND):
        quarter = piece % 4
        out[piece // 4, :, quarter * LANES : (quarter + 1) * LANES] = rows[
            piece * 48 : piece * 48 + 32, :
        ]
    lower = lax.broadcasted_iota(jnp.int32, (16, LANES), 1) < 64
    for half in range(8):
        lanes = slice((half % 4) * LANES, (half % 4 + 1) * LANES)
        even = rows[2 * half * 48 + 32 : 2 * half * 48 + 48, :]
        odd = rows[(2 * half + 1) * 48 + 32 : (2 * half + 1) * 48 + 48, :]
        out[4 + half // 4, 0:16, lanes] = jnp.where(lower, even, pltpu.roll(odd, 64, 1))
        out[4 + half // 4, 16:32, lanes] = jnp.where(lower, pltpu.roll(even, 64, 1), odd)


def whole():
    return pl.BlockSpec(memory_space=pltpu.VMEM)


def scalar():
    return pl.BlockSpec(memory_space=pltpu.SMEM)


def call(kernel, name, shape, specs, scratch=()):
    return pl.pallas_call(
        kernel,
        name=name,
        out_shape=jax.ShapeDtypeStruct(shape, f32),
        in_specs=specs,
        out_specs=whole(),
        scratch_shapes=list(scratch),
        compiler_params=pltpu.CompilerParams(vmem_limit_bytes=48 << 20),
    )


def do_pack(psi, potential):
    return call(pack_kernel, "pack", (TILE * 8 * DEPTH, LANES), [whole()] * 2)(psi, potential)


def do_filter(rows):
    strip = np.stack(split_constant(plane_matrix()[:LANES]))
    layers = np.stack(split_constant(layer_matrix()))
    return call(
        filter_kernel,
        "filter",
        (2 * NB, LANES),
        [whole()] * 3,
        [pltpu.VMEM((4 * NZ, LANES), f32), pltpu.VMEM((2, CELLS, CELLS), bf16)],
    )(rows, jnp.asarray(strip), jnp.asarray(layers))


def do_gram(core, rows):
    half = jax.ShapeDtypeStruct((NB, LANES), f32)
    return pl.pallas_call(
        gram_kernel,
        name="gram",
        out_shape=(half, half),
        in_specs=[scalar(), whole()],
        out_specs=(whole(), whole()),
        compiler_params=pltpu.CompilerParams(vmem_limit_bytes=48 << 20),
    )(core, rows)


def do_sum(parts, copies, scale):
    return call(sum_kernel(scale), "sum", (copies,) + parts.shape[1:], [whole()])(parts)


def do_solve(core, mine, other, rows):
    return call(
        solve_kernel,
        "solve",
        (BAND * 48, LANES),
        [scalar(), whole(), whole(), whole()],
        [
            pltpu.VMEM((4, NB, LANES), f32),
            pltpu.VMEM((NB, 2 * LANES), f32),
            pltpu.VMEM((4, LANES, LANES), f32),
            pltpu.VMEM((4, 2, LANES, LANES), bf16),
            pltpu.VMEM((4, 2, LANES, LANES), bf16),
            pltpu.VMEM((8, LANES), f32),
        ],
    )(core, mine, other, rows)


def do_unpack(rows):
    return call(unpack_kernel, "unpack", (DEPTH, TILE, CELLS), [whole()])(rows)


def exchange(rows, axis, parts):
    shaped = rows.reshape(parts, rows.shape[0] // parts, LANES)
    return lax.all_to_all(shaped, axis, 0, 0).reshape(rows.shape)


def swap_cores(value):
    return lax.ppermute(value, "core", [(0, 1), (1, 0)])


def gram_sum(keep, send):
    depth = SIDES[3]
    half = (keep + swap_cores(send)).reshape(IN_PLANE, NB // IN_PLANE, LANES)
    half = do_sum(lax.all_to_all(half, PLANE, 0, 0), depth, 1.0)
    half = do_sum(lax.all_to_all(half, "z", 0, 0), IN_PLANE, 1.0 / NPTS)
    return lax.all_to_all(half, PLANE, 0, 0).reshape(NB, LANES)


def shards(psi, potential):
    core = lax.axis_index("core").astype(jnp.int32).reshape(1)
    psi, core = lax.optimization_barrier((psi, core))
    bands = exchange(do_pack(jnp.transpose(psi, (1, 0, 2)), potential), LAYERS, DOM)
    points = exchange(do_filter(bands), ALL, NB)
    gram = gram_sum(*do_gram(core, points))
    result = exchange(do_solve(core, gram, swap_cores(gram), points), BANDS, BAND)
    return jnp.transpose(do_unpack(result), (1, 0, 2))


def solution(mesh):
    split = Mesh(np.asarray(mesh.devices).reshape(SIDES), NAMES)
    bands = P(BANDS, LAYERS, None)
    return jax.shard_map(
        shards, mesh=split, in_specs=(bands, P(LAYERS, None)), out_specs=bands, check_vma=False
    )
```

```python
import jax
import jax.numpy as jnp
import numpy as np
from jax import lax
from jax.experimental import pallas as pl
from jax.experimental.pallas import tpu as pltpu
from jax.sharding import Mesh, PartitionSpec as P

NB = 512
LX = 32
LY = 16
NZ = 192
CELLS = LX * LY
NPTS = NZ * CELLS
DEG = 4
DOM = 32
BAND = 16
TILE = NB // BAND
DEPTH = NZ // DOM
LANES = 128
SIDES = (8, 2, 2, 8, 2)
NAMES = ("y", "xh", "core", "z", "xl")
LAYERS = ("y", "xh", "core")
BANDS = ("z", "xl")
ALL = BANDS + LAYERS
PLANE = ("y", "xh", "xl")
IN_PLANE = 32

COEF = (
    -5369.0 / 1800.0,
    12.0 / 7.0,
    -15.0 / 56.0,
    10.0 / 189.0,
    -1.0 / 112.0,
    2.0 / 1925.0,
    -1.0 / 16632.0,
)
INV_SPACING2 = 4.0
CENTRE = 24.0
HALF_WIDTH = 20.0

HIGHEST = lax.Precision.HIGHEST
f32 = jnp.float32
bf16 = jnp.bfloat16


def split_constant(matrix):
    pieces = []
    rest = matrix.astype(np.float64)
    for _ in range(2):
        piece = rest.astype(np.float32).astype(bf16)
        pieces.append(piece)
        rest = rest - piece.astype(np.float64)
    return pieces


def plane_matrix():
    out = np.zeros((CELLS, CELLS))
    scale = -0.5 * INV_SPACING2 / HALF_WIDTH
    for y in range(LY):
        for x in range(LX):
            row = y * LX + x
            out[row, row] += scale * 3.0 * COEF[0] - CENTRE / HALF_WIDTH
            for k in range(1, 7):
                for step in (k, -k):
                    out[row, y * LX + (x + step) % LX] += scale * COEF[k]
                    out[row, (y + step) % LY * LX + x] += scale * COEF[k]
    return out


def layer_matrix():
    out = np.zeros((NZ, NZ))
    scale = -0.5 * INV_SPACING2 / HALF_WIDTH
    for k in range(1, 7):
        out += scale * COEF[k] * (np.eye(NZ, k=k) + np.eye(NZ, k=-k))
    return out


def split_value(value):
    high = value.astype(bf16)
    return high, (value - high.astype(f32)).astype(bf16)


def dot_split(left, right):
    def dot(a, b):
        return jnp.dot(a, b, preferred_element_type=f32)

    return (dot(left[0], right[1]) + dot(left[1], right[0])) + dot(left[0], right[0])


def pack_kernel(psi, potential, out):
    for layer in range(DEPTH):
        for quarter in range(4):
            lanes = slice(quarter * LANES, (quarter + 1) * LANES)
            row = layer * 8 + quarter
            out[pl.ds(row, TILE, stride=8 * DEPTH), :] = psi[layer, :, lanes]
            out[pl.ds(row + 4, TILE, stride=8 * DEPTH), :] = jnp.broadcast_to(
                potential[layer : layer + 1, lanes] * (1.0 / HALF_WIDTH), (TILE, LANES)
            )


def filter_kernel(rows, strip, m_layer, out, scratch, m_plane):
    for piece in range(2):
        for i in range(4):
            for j in range(4):
                at = (j - i) % 4 * LANES
                m_plane[piece, i * LANES : (i + 1) * LANES, j * LANES : (j + 1) * LANES] = strip[
                    piece, :, at : at + LANES
                ]
    start = jnp.concatenate([rows[pl.ds(q, NZ, stride=8), :] for q in range(4)], axis=1)
    potential = jnp.concatenate([rows[pl.ds(4 + q, NZ, stride=8), :] for q in range(4)], axis=1)
    plane = (m_plane[0], m_plane[1])
    layers = (m_layer[0], m_layer[1])

    def apply(values):
        pieces = split_value(values)
        return dot_split(pieces, plane) + dot_split(layers, pieces) + potential * values

    previous = start
    current = apply(start)
    for _ in range(1, DEG):
        previous, current = current, 2.0 * apply(current) - previous
    norm = jnp.sum(jnp.sum(current * current, axis=0, keepdims=True), axis=1, keepdims=True) * (
        1.0 / NPTS
    )
    for quarter in range(4):
        scratch[quarter * NZ : (quarter + 1) * NZ, :] = current[
            :, quarter * LANES : (quarter + 1) * LANES
        ]
    lane = lax.broadcasted_iota(jnp.int32, (DOM, LANES), 1)
    norms = jnp.broadcast_to(norm, (DOM, LANES))
    for piece in range(BAND):
        first = scratch[pl.ds((piece % 4) * NZ + piece // 4, DOM, stride=DEPTH), :]
        half = piece // 2
        second = scratch[pl.ds((half % 4) * NZ + 4 + half // 4, DOM, stride=DEPTH), :]
        if piece % 2:
            second = pltpu.roll(second, 64, 1)
        out[pl.ds(piece * 2 * DOM, DOM, stride=2), :] = first
        out[pl.ds(piece * 2 * DOM + 1, DOM, stride=2), :] = jnp.where(lane < 64, second, norms)


def points_of(rows):
    first = rows[pl.ds(0, NB, stride=2), :]
    second = rows[pl.ds(1, NB, stride=2), :]
    lane = lax.broadcasted_iota(jnp.int32, (NB, LANES), 1)
    return first, jnp.where(lane < 64, second, 0.0), second


def dot_nt(a, b):
    return lax.dot_general(
        a, b, (((1,), (1,)), ((), ())), precision=HIGHEST, preferred_element_type=f32
    )


def gram_kernel(core, rows, keep, send):
    first, second, _ = points_of(rows)
    points = jnp.concatenate([first, second], axis=1)
    low, high = points[:256], points[256:]
    row = lax.broadcasted_iota(jnp.int32, (256, 256), 0)
    col = lax.broadcasted_iota(jnp.int32, (256, 256), 1)
    folded = jnp.where(col <= row, dot_nt(low, low), dot_nt(high, high))
    below = dot_nt(high, low)
    first = core[0] == 0
    for half in range(2):
        lanes = slice(half * LANES, (half + 1) * LANES)
        at = slice(half * 256, (half + 1) * 256)
        keep[at, :] = jnp.where(first, folded[:, lanes], below[:, lanes])
        send[at, :] = jnp.where(first, below[:, lanes], folded[:, lanes])


def sum_kernel(scale):
    def kernel(parts, out):
        total = jnp.sum(parts[...], axis=0) * scale
        out[...] = jnp.broadcast_to(total[None], out.shape)

    return kernel


def invert_block(m, y_ref, ones, work):
    full = (8, LANES)
    sub = lax.broadcasted_iota(jnp.int32, full, 0)
    lane = lax.broadcasted_iota(jnp.int32, full, 1)

    def row(value, u):
        return jnp.broadcast_to(value[u : u + 1, :], full)

    def column(value, at):
        return jnp.broadcast_to(value[:, at : at + 1], full)

    def total(terms):
        return ((terms[0] + terms[1]) + (terms[2] + terms[3])) + (
            (terms[4] + terms[5]) + (terms[6] + terms[7])
        )

    def later(q, base, inside):
        def update():
            here = slice(8 * q, 8 * q + 8)
            d = m[here, :]
            terms = [
                column(d, base + t) * y_ref[pl.ds(base + t, 8, stride=0), :] for t in range(8)
            ]
            m[here, :] = jnp.where(inside, 0.0, d) + total(terms)

        return update

    def some(calls, steps_left):
        for _ in range(-(-len(calls) // steps_left)):
            calls.pop(0)()

    v = m[0:8, :]
    waiting = []
    for panel in range(16):
        base = 8 * panel
        inside = (lane >= base) & (lane < base + 8)
        a = [column(v, base + t) * ones for t in range(8)]
        v = jnp.where(inside, jnp.where(lane - base == sub, 1.0, 0.0), v)
        v_rows = [row(v, u) for u in range(8)]
        lower = [jnp.zeros(full, f32) for _ in range(7)]
        scale = jnp.zeros(full, f32)
        pivots = [row(a[0], j) for j in range(8)]
        for k in range(8):
            here = sub == k
            ahead = [row(a[k], j) for j in range(k)] + pivots[k:]
            if k == 7:
                masked = [jnp.where(here, 0.0, a[u]) for u in range(7)]
                y = total([masked[u] * v_rows[u] for u in range(7)] + [jnp.zeros(full, f32)])
                rest = v_rows[7] - total(
                    [ahead[u] * v_rows[u] for u in range(7)] + [jnp.zeros(full, f32)]
                )
            root = lax.rsqrt(ahead[k])
            inverse = root * root
            if k < 7:
                pivots = [None] * (k + 1) + [
                    row(a[k + 1], j) - (ahead[k + 1] * ahead[j]) * inverse for j in range(k + 1, 8)
                ]
            for t in range(k):
                lower[t] = jnp.where(here, a[t], lower[t])
            scale = jnp.where(here, root, scale)
            swept = jnp.where(here, -inverse, a[k] * inverse)
            if k < 7:
                for j in range(8):
                    if j != k:
                        a[j] = jnp.where(here, 0.0, a[j]) - swept * ahead[j]
                a[k] = swept
                if k > 0:
                    some(waiting, 7 - k)
            else:
                y = y + swept * rest
        waiting = []
        if panel < 15:
            y_ref[base : base + 8, :] = y
            d = m[base + 8 : base + 16, :]
            terms = [column(d, base + t) * row(y, t) for t in range(8)]
            following = jnp.where(inside, 0.0, d) + total(terms)
            waiting = [later(q, base, inside) for q in range(panel + 2, 16)]
        done = v
        for t in range(7):
            done = done - lower[t] * v_rows[t]
        m[base : base + 8, :] = jnp.where(lane < base + 8, done * scale, 0.0)
        if panel < 15:
            v = following
        some(work, 16 - panel)


def solve_kernel(core, mine, other, rows, out, s_ref, x_ref, blocks, panels, inverses, y_ref, ones_ref):
    first, second, raw = points_of(rows)
    x_ref[:, :LANES] = first
    x_ref[:, LANES:] = second
    ones_ref[...] = jnp.ones((8, LANES), f32)
    swap = core[0] == 0
    folded = jnp.where(swap, mine[...], other[...])
    folded = jnp.concatenate([folded[:256], folded[256:]], axis=1)
    flipped = folded.T
    row = lax.broadcasted_iota(jnp.int32, (256, 256), 0)
    col = lax.broadcasted_iota(jnp.int32, (256, 256), 1)
    low = jnp.where(col <= row, folded, flipped)
    norms = jnp.broadcast_to(raw[256:, LANES - 1 : LANES], (256, 256))
    high = jnp.where(col == row, norms, jnp.where(col > row, folded, flipped))
    s_ref[0, :256, :] = low[:, :LANES]
    s_ref[1, :256, :] = low[:, LANES:]
    s_ref[0, 256:, :] = jnp.where(swap, other[:256, :], mine[:256, :])
    s_ref[1, 256:, :] = jnp.where(swap, other[256:, :], mine[256:, :])
    s_ref[2, 256:, :] = high[:, :LANES]
    s_ref[3, 256:, :] = high[:, LANES:]

    def at(i):
        return slice(i * LANES, (i + 1) * LANES)

    def split_dot(left, right, dims):
        def dot(a, b):
            return lax.dot_general(a, b, (dims, ((), ())), preferred_element_type=f32)

        return (dot(left[0], right[1]) + dot(left[1], right[0])) + dot(left[0], right[0])

    nt, nn = ((1,), (1,)), ((1,), (0,))

    def pieces(ref, i):
        return ref[i, 0], ref[i, 1]

    def put(ref, i, value):
        ref[i, 0], ref[i, 1] = split_value(value)

    def form_panel(j, i):
        put(panels, i, split_dot(split_value(s_ref[j, at(i), :]), pieces(inverses, j), nt))

    def update_s(k, i):
        s_ref[k, at(i), :] = s_ref[k, at(i), :] - split_dot(
            pieces(panels, i), pieces(panels, k), nt
        )

    def solve_x(j):
        x_ref[at(j), :] = split_dot(pieces(inverses, j), split_value(x_ref[at(j), :]), nn)

    def update_x(j, i):
        x_ref[at(i), :] = x_ref[at(i), :] - split_dot(
            pieces(panels, i), split_value(x_ref[at(j), :]), nn
        )

    ones = ones_ref[...]
    work = []
    blocks[0] = s_ref[0, at(0), :]
    for j in range(4):
        invert_block(blocks.at[j], y_ref, ones, work)
        put(inverses, j, blocks[j])
        work = []
        if j < 3:
            form_panel(j, j + 1)
            blocks[j + 1] = s_ref[j + 1, at(j + 1), :] - split_dot(
                pieces(panels, j + 1), pieces(panels, j + 1), nt
            )
            for i in range(j + 2, 4):
                work.append(lambda j=j, i=i: form_panel(j, i))
                work.append(lambda k=j + 1, i=i: update_s(k, i))
            for k in range(j + 2, 4):
                for i in range(k, 4):
                    work.append(lambda k=k, i=i: update_s(k, i))
        work.append(lambda j=j: solve_x(j))
        for i in range(j + 1, 4):
            work.append(lambda j=j, i=i: update_x(j, i))
    for call_ in work:
        call_()
    for tile in range(BAND):
        at_ = tile * TILE
        out[tile * 48 : tile * 48 + 32, :] = x_ref[at_ : at_ + TILE, :LANES]
        out[tile * 48 + 32 : tile * 48 + 48, :] = x_ref[at_ : at_ + 16, LANES:] + pltpu.roll(
            x_ref[at_ + 16 : at_ + 32, LANES:], 64, 1
        )


def unpack_kernel(rows, out):
    for piece in range(BAND):
        quarter = piece % 4
        out[piece // 4, :, quarter * LANES : (quarter + 1) * LANES] = rows[
            piece * 48 : piece * 48 + 32, :
        ]
    lower = lax.broadcasted_iota(jnp.int32, (16, LANES), 1) < 64
    for half in range(8):
        lanes = slice((half % 4) * LANES, (half % 4 + 1) * LANES)
        even = rows[2 * half * 48 + 32 : 2 * half * 48 + 48, :]
        odd = rows[(2 * half + 1) * 48 + 32 : (2 * half + 1) * 48 + 48, :]
        out[4 + half // 4, 0:16, lanes] = jnp.where(lower, even, pltpu.roll(odd, 64, 1))
        out[4 + half // 4, 16:32, lanes] = jnp.where(lower, pltpu.roll(even, 64, 1), odd)


def whole():
    return pl.BlockSpec(memory_space=pltpu.VMEM)


def scalar():
    return pl.BlockSpec(memory_space=pltpu.SMEM)


def call(kernel, name, shape, specs, scratch=()):
    return pl.pallas_call(
        kernel,
        name=name,
        out_shape=jax.ShapeDtypeStruct(shape, f32),
        in_specs=specs,
        out_specs=whole(),
        scratch_shapes=list(scratch),
        compiler_params=pltpu.CompilerParams(vmem_limit_bytes=48 << 20),
    )


def do_pack(psi, potential):
    return call(pack_kernel, "pack", (TILE * 8 * DEPTH, LANES), [whole()] * 2)(psi, potential)


def do_filter(rows):
    strip = np.stack(split_constant(plane_matrix()[:LANES]))
    layers = np.stack(split_constant(layer_matrix()))
    return call(
        filter_kernel,
        "filter",
        (2 * NB, LANES),
        [whole()] * 3,
        [pltpu.VMEM((4 * NZ, LANES), f32), pltpu.VMEM((2, CELLS, CELLS), bf16)],
    )(rows, jnp.asarray(strip), jnp.asarray(layers))


def do_gram(core, rows):
    half = jax.ShapeDtypeStruct((NB, LANES), f32)
    return pl.pallas_call(
        gram_kernel,
        name="gram",
        out_shape=(half, half),
        in_specs=[scalar(), whole()],
        out_specs=(whole(), whole()),
        compiler_params=pltpu.CompilerParams(vmem_limit_bytes=48 << 20),
    )(core, rows)


def do_sum(parts, copies, scale):
    return call(sum_kernel(scale), "sum", (copies,) + parts.shape[1:], [whole()])(parts)


def do_solve(core, mine, other, rows):
    return call(
        solve_kernel,
        "solve",
        (BAND * 48, LANES),
        [scalar(), whole(), whole(), whole()],
        [
            pltpu.VMEM((4, NB, LANES), f32),
            pltpu.VMEM((NB, 2 * LANES), f32),
            pltpu.VMEM((4, LANES, LANES), f32),
            pltpu.VMEM((4, 2, LANES, LANES), bf16),
            pltpu.VMEM((4, 2, LANES, LANES), bf16),
            pltpu.VMEM((LANES, LANES), f32),
            pltpu.VMEM((8, LANES), f32),
        ],
    )(core, mine, other, rows)


def do_unpack(rows):
    return call(unpack_kernel, "unpack", (DEPTH, TILE, CELLS), [whole()])(rows)


def exchange(rows, axis, parts):
    shaped = rows.reshape(parts, rows.shape[0] // parts, LANES)
    return lax.all_to_all(shaped, axis, 0, 0).reshape(rows.shape)


def swap_cores(value):
    return lax.ppermute(value, "core", [(0, 1), (1, 0)])


def gram_sum(keep, send):
    depth = SIDES[3]
    half = (keep + swap_cores(send)).reshape(IN_PLANE, NB // IN_PLANE, LANES)
    half = do_sum(lax.all_to_all(half, PLANE, 0, 0), depth, 1.0)
    half = do_sum(lax.all_to_all(half, "z", 0, 0), IN_PLANE, 1.0 / NPTS)
    return lax.all_to_all(half, PLANE, 0, 0).reshape(NB, LANES)


def shards(psi, potential):
    core = lax.axis_index("core").astype(jnp.int32).reshape(1)
    psi, core = lax.optimization_barrier((psi, core))
    bands = exchange(do_pack(jnp.transpose(psi, (1, 0, 2)), potential), LAYERS, DOM)
    points = exchange(do_filter(bands), ALL, NB)
    gram = gram_sum(*do_gram(core, points))
    result = exchange(do_solve(core, gram, swap_cores(gram), points), BANDS, BAND)
    return jnp.transpose(do_unpack(result), (1, 0, 2))


def solution(mesh):
    split = Mesh(np.asarray(mesh.devices).reshape(SIDES), NAMES)
    bands = P(BANDS, LAYERS, None)
    return jax.shard_map(
        shards, mesh=split, in_specs=(bands, P(LAYERS, None)), out_specs=bands, check_vma=False
    )
```

```python
import jax
import jax.numpy as jnp
import numpy as np
from jax import lax
from jax.experimental import pallas as pl
from jax.experimental.pallas import tpu as pltpu
from jax.sharding import Mesh, PartitionSpec as P

NB = 512
LX = 32
LY = 16
NZ = 192
CELLS = LX * LY
NPTS = NZ * CELLS
DEG = 4
DOM = 32
BAND = 16
TILE = NB // BAND
DEPTH = NZ // DOM
LANES = 128
SIDES = (8, 2, 2, 8, 2)
NAMES = ("y", "xh", "core", "z", "xl")
LAYERS = ("y", "xh", "core")
BANDS = ("z", "xl")
ALL = BANDS + LAYERS
PLANE = ("y", "xh", "xl")
IN_PLANE = 32

COEF = (
    -5369.0 / 1800.0,
    12.0 / 7.0,
    -15.0 / 56.0,
    10.0 / 189.0,
    -1.0 / 112.0,
    2.0 / 1925.0,
    -1.0 / 16632.0,
)
INV_SPACING2 = 4.0
CENTRE = 24.0
HALF_WIDTH = 20.0

f32 = jnp.float32
bf16 = jnp.bfloat16


def split_constant(matrix):
    pieces = []
    rest = matrix.astype(np.float64)
    for _ in range(2):
        piece = rest.astype(np.float32).astype(bf16)
        pieces.append(piece)
        rest = rest - piece.astype(np.float64)
    return pieces


def plane_matrix():
    out = np.zeros((CELLS, CELLS))
    scale = -0.5 * INV_SPACING2 / HALF_WIDTH
    for y in range(LY):
        for x in range(LX):
            row = y * LX + x
            out[row, row] += scale * 3.0 * COEF[0] - CENTRE / HALF_WIDTH
            for k in range(1, 7):
                for step in (k, -k):
                    out[row, y * LX + (x + step) % LX] += scale * COEF[k]
                    out[row, (y + step) % LY * LX + x] += scale * COEF[k]
    return out


def layer_matrix():
    out = np.zeros((NZ, NZ))
    scale = -0.5 * INV_SPACING2 / HALF_WIDTH
    for k in range(1, 7):
        out += scale * COEF[k] * (np.eye(NZ, k=k) + np.eye(NZ, k=-k))
    return out


def split_value(value):
    high = value.astype(bf16)
    return high, (value - high.astype(f32)).astype(bf16)


NN = ((1,), (0,))
NT = ((1,), (1,))


def dot_split(left, right, dims):
    a = jnp.concatenate([left[0], left[1], left[0]], axis=dims[0][0])
    b = jnp.concatenate([right[1], right[0], right[0]], axis=dims[1][0])
    return lax.dot_general(a, b, (dims, ((), ())), preferred_element_type=f32)


def dot_apart(left, right):
    def dot(a, b):
        return jnp.dot(a, b, preferred_element_type=f32)

    return (dot(left[0], right[1]) + dot(left[1], right[0])) + dot(left[0], right[0])


def pack_kernel(psi, potential, out):
    for layer in range(DEPTH):
        for quarter in range(4):
            lanes = slice(quarter * LANES, (quarter + 1) * LANES)
            row = layer * 8 + quarter
            out[pl.ds(row, TILE, stride=8 * DEPTH), :] = psi[layer, :, lanes]
            out[pl.ds(row + 4, TILE, stride=8 * DEPTH), :] = jnp.broadcast_to(
                potential[layer : layer + 1, lanes], (TILE, LANES)
            )


def filter_kernel(rows, strip, m_layer, out, scratch, m_plane):
    for piece in range(2):
        for i in range(4):
            for j in range(4):
                at = (j - i) % 4 * LANES
                m_plane[piece, i * LANES : (i + 1) * LANES, j * LANES : (j + 1) * LANES] = strip[
                    piece, :, at : at + LANES
                ]
    start = jnp.concatenate([rows[pl.ds(q, NZ, stride=8), :] for q in range(4)], axis=1)
    potential = jnp.concatenate([rows[pl.ds(4 + q, NZ, stride=8), :] for q in range(4)], axis=1)
    plane = (m_plane[0], m_plane[1])
    layers = (m_layer[0], m_layer[1])

    def apply(values):
        pieces = split_value(values)
        return dot_apart(pieces, plane) + dot_apart(layers, pieces) + potential * values

    previous = start
    current = apply(start)
    for _ in range(1, DEG):
        previous, current = current, 2.0 * apply(current) - previous
    norm = jnp.sum(jnp.sum(current * current, axis=0, keepdims=True), axis=1, keepdims=True) * (
        1.0 / NPTS
    )
    for quarter in range(4):
        scratch[quarter * NZ : (quarter + 1) * NZ, :] = current[
            :, quarter * LANES : (quarter + 1) * LANES
        ]
    lane = lax.broadcasted_iota(jnp.int32, (DOM, LANES), 1)
    norms = jnp.broadcast_to(norm, (DOM, LANES))
    for piece in range(BAND):
        first = scratch[pl.ds((piece % 4) * NZ + piece // 4, DOM, stride=DEPTH), :]
        half = piece // 2
        second = scratch[pl.ds((half % 4) * NZ + 4 + half // 4, DOM, stride=DEPTH), :]
        if piece % 2:
            second = pltpu.roll(second, 64, 1)
        out[pl.ds(piece * 2 * DOM, DOM, stride=2), :] = first
        out[pl.ds(piece * 2 * DOM + 1, DOM, stride=2), :] = jnp.where(lane < 64, second, norms)


def points_of(rows):
    first = rows[pl.ds(0, NB, stride=2), :]
    second = rows[pl.ds(1, NB, stride=2), :]
    lane = lax.broadcasted_iota(jnp.int32, (NB, LANES), 1)
    return first, jnp.where(lane < 64, second, 0.0), second


def gram_kernel(core, rows, keep, send):
    first, second, _ = points_of(rows)
    points = split_value(jnp.concatenate([first, second], axis=1))
    low, high = [p[:256] for p in points], [p[256:] for p in points]
    row = lax.broadcasted_iota(jnp.int32, (256, 256), 0)
    col = lax.broadcasted_iota(jnp.int32, (256, 256), 1)
    folded = jnp.where(col <= row, dot_split(low, low, NT), dot_split(high, high, NT))
    below = dot_split(high, low, NT)
    first = core[0] == 0
    for half in range(2):
        lanes = slice(half * LANES, (half + 1) * LANES)
        at = slice(half * 256, (half + 1) * 256)
        keep[at, :] = jnp.where(first, folded[:, lanes], below[:, lanes])
        send[at, :] = jnp.where(first, below[:, lanes], folded[:, lanes])


def sum_kernel(scale):
    def kernel(parts, out):
        total = jnp.sum(parts[...], axis=0) * scale
        out[...] = jnp.broadcast_to(total[None], out.shape)

    return kernel


def invert_block(m, y_ref, ones, work):
    full = (8, LANES)
    sub = lax.broadcasted_iota(jnp.int32, full, 0)
    lane = lax.broadcasted_iota(jnp.int32, full, 1)

    def row(value, u):
        return jnp.broadcast_to(value[u : u + 1, :], full)

    def column(value, at):
        return jnp.broadcast_to(value[:, at : at + 1], full)

    def total(terms):
        return ((terms[0] + terms[1]) + (terms[2] + terms[3])) + (
            (terms[4] + terms[5]) + (terms[6] + terms[7])
        )

    def later(q, base, inside):
        def update():
            here = slice(8 * q, 8 * q + 8)
            d = m[here, :]
            terms = [
                column(d, base + t) * y_ref[pl.ds(base + t, 8, stride=0), :] for t in range(8)
            ]
            m[here, :] = jnp.where(inside, 0.0, d) + total(terms)

        return update

    def some(calls, steps_left):
        for _ in range(-(-len(calls) // steps_left)):
            calls.pop(0)()

    v = m[0:8, :]
    waiting = []
    for panel in range(16):
        base = 8 * panel
        inside = (lane >= base) & (lane < base + 8)
        a = [column(v, base + t) * ones for t in range(8)]
        v = jnp.where(inside, jnp.where(lane - base == sub, 1.0, 0.0), v)
        v_rows = [row(v, u) for u in range(8)]
        lower = [jnp.zeros(full, f32) for _ in range(7)]
        scale = jnp.zeros(full, f32)
        pivots = [row(a[0], j) for j in range(8)]
        for k in range(8):
            here = sub == k
            ahead = [row(a[k], j) for j in range(k)] + pivots[k:]
            if k == 7:
                masked = [jnp.where(here, 0.0, a[u]) for u in range(7)]
                y = total([masked[u] * v_rows[u] for u in range(7)] + [jnp.zeros(full, f32)])
                rest = v_rows[7] - total(
                    [ahead[u] * v_rows[u] for u in range(7)] + [jnp.zeros(full, f32)]
                )
            root = lax.rsqrt(ahead[k])
            inverse = root * root
            if k < 7:
                pivots = [None] * (k + 1) + [
                    row(a[k + 1], j) - (ahead[k + 1] * ahead[j]) * inverse for j in range(k + 1, 8)
                ]
            for t in range(k):
                lower[t] = jnp.where(here, a[t], lower[t])
            scale = jnp.where(here, root, scale)
            swept = jnp.where(here, -inverse, a[k] * inverse)
            if k < 7:
                for j in range(8):
                    if j != k:
                        a[j] = jnp.where(here, 0.0, a[j]) - swept * ahead[j]
                a[k] = swept
                if k > 0:
                    some(waiting, 7 - k)
            else:
                y = y + swept * rest
        waiting = []
        if panel < 15:
            y_ref[base : base + 8, :] = y
            d = m[base + 8 : base + 16, :]
            terms = [column(d, base + t) * row(y, t) for t in range(8)]
            following = jnp.where(inside, 0.0, d) + total(terms)
            waiting = [later(q, base, inside) for q in range(panel + 2, 16)]
        done = v
        for t in range(7):
            done = done - lower[t] * v_rows[t]
        m[base : base + 8, :] = jnp.where(lane < base + 8, done * scale, 0.0)
        if panel < 15:
            v = following
        some(work, 16 - panel)


def solve_kernel(core, mine, other, rows, out, s_ref, x_ref, blocks, panels, inverses, y_ref, ones_ref):
    first, second, raw = points_of(rows)
    x_ref[:, :LANES] = first
    x_ref[:, LANES:] = second
    ones_ref[...] = jnp.ones((8, LANES), f32)
    swap = core[0] == 0
    folded = jnp.where(swap, mine[...], other[...])
    folded = jnp.concatenate([folded[:256], folded[256:]], axis=1)
    flipped = folded.T
    row = lax.broadcasted_iota(jnp.int32, (256, 256), 0)
    col = lax.broadcasted_iota(jnp.int32, (256, 256), 1)
    low = jnp.where(col <= row, folded, flipped)
    norms = jnp.broadcast_to(raw[256:, LANES - 1 : LANES], (256, 256))
    high = jnp.where(col == row, norms, jnp.where(col > row, folded, flipped))
    s_ref[0, :256, :] = low[:, :LANES]
    s_ref[1, :256, :] = low[:, LANES:]
    s_ref[0, 256:, :] = jnp.where(swap, other[:256, :], mine[:256, :])
    s_ref[1, 256:, :] = jnp.where(swap, other[256:, :], mine[256:, :])
    s_ref[2, 256:, :] = high[:, :LANES]
    s_ref[3, 256:, :] = high[:, LANES:]

    def at(i):
        return slice(i * LANES, (i + 1) * LANES)

    def pieces(ref, i):
        return ref[i, 0], ref[i, 1]

    def put(ref, i, value):
        ref[i, 0], ref[i, 1] = split_value(value)

    def form_panel(j, i):
        put(panels, i, dot_split(split_value(s_ref[j, at(i), :]), pieces(inverses, j), NT))

    def update_s(k, i):
        s_ref[k, at(i), :] = s_ref[k, at(i), :] - dot_split(
            pieces(panels, i), pieces(panels, k), NT
        )

    def solve_x(j):
        x_ref[at(j), :] = dot_split(pieces(inverses, j), split_value(x_ref[at(j), :]), NN)

    def update_x(j, i):
        x_ref[at(i), :] = x_ref[at(i), :] - dot_split(
            pieces(panels, i), split_value(x_ref[at(j), :]), NN
        )

    ones = ones_ref[...]
    work = []
    blocks[0] = s_ref[0, at(0), :]
    for j in range(4):
        invert_block(blocks.at[j], y_ref, ones, work)
        put(inverses, j, blocks[j])
        work = []
        if j < 3:
            form_panel(j, j + 1)
            blocks[j + 1] = s_ref[j + 1, at(j + 1), :] - dot_split(
                pieces(panels, j + 1), pieces(panels, j + 1), NT
            )
            for i in range(j + 2, 4):
                work.append(lambda j=j, i=i: form_panel(j, i))
                work.append(lambda k=j + 1, i=i: update_s(k, i))
            for k in range(j + 2, 4):
                for i in range(k, 4):
                    work.append(lambda k=k, i=i: update_s(k, i))
        work.append(lambda j=j: solve_x(j))
        for i in range(j + 1, 4):
            work.append(lambda j=j, i=i: update_x(j, i))
    for call_ in work:
        call_()
    for tile in range(BAND):
        at_ = tile * TILE
        out[tile * 48 : tile * 48 + 32, :] = x_ref[at_ : at_ + TILE, :LANES]
        out[tile * 48 + 32 : tile * 48 + 48, :] = x_ref[at_ : at_ + 16, LANES:] + pltpu.roll(
            x_ref[at_ + 16 : at_ + 32, LANES:], 64, 1
        )


def unpack_kernel(rows, out):
    for piece in range(BAND):
        quarter = piece % 4
        out[piece // 4, :, quarter * LANES : (quarter + 1) * LANES] = rows[
            piece * 48 : piece * 48 + 32, :
        ]
    lower = lax.broadcasted_iota(jnp.int32, (16, LANES), 1) < 64
    for half in range(8):
        lanes = slice((half % 4) * LANES, (half % 4 + 1) * LANES)
        even = rows[2 * half * 48 + 32 : 2 * half * 48 + 48, :]
        odd = rows[(2 * half + 1) * 48 + 32 : (2 * half + 1) * 48 + 48, :]
        out[4 + half // 4, 0:16, lanes] = jnp.where(lower, even, pltpu.roll(odd, 64, 1))
        out[4 + half // 4, 16:32, lanes] = jnp.where(lower, pltpu.roll(even, 64, 1), odd)


def whole():
    return pl.BlockSpec(memory_space=pltpu.VMEM)


def scalar():
    return pl.BlockSpec(memory_space=pltpu.SMEM)


def call(kernel, name, shape, specs, scratch=()):
    return pl.pallas_call(
        kernel,
        name=name,
        out_shape=jax.ShapeDtypeStruct(shape, f32),
        in_specs=specs,
        out_specs=whole(),
        scratch_shapes=list(scratch),
        compiler_params=pltpu.CompilerParams(vmem_limit_bytes=48 << 20),
    )


def do_pack(psi, potential):
    return call(pack_kernel, "pack", (TILE * 8 * DEPTH, LANES), [whole()] * 2)(psi, potential)


def do_filter(rows):
    strip = np.stack(split_constant(plane_matrix()[:LANES]))
    layers = np.stack(split_constant(layer_matrix()))
    return call(
        filter_kernel,
        "filter",
        (2 * NB, LANES),
        [whole()] * 3,
        [pltpu.VMEM((4 * NZ, LANES), f32), pltpu.VMEM((2, CELLS, CELLS), bf16)],
    )(rows, jnp.asarray(strip), jnp.asarray(layers))


def do_gram(core, rows):
    half = jax.ShapeDtypeStruct((NB, LANES), f32)
    return pl.pallas_call(
        gram_kernel,
        name="gram",
        out_shape=(half, half),
        in_specs=[scalar(), whole()],
        out_specs=(whole(), whole()),
        compiler_params=pltpu.CompilerParams(vmem_limit_bytes=48 << 20),
    )(core, rows)


def do_sum(parts, copies, scale):
    return call(sum_kernel(scale), "sum", (copies,) + parts.shape[1:], [whole()])(parts)


def do_solve(core, mine, other, rows):
    return call(
        solve_kernel,
        "solve",
        (BAND * 48, LANES),
        [scalar(), whole(), whole(), whole()],
        [
            pltpu.VMEM((4, NB, LANES), f32),
            pltpu.VMEM((NB, 2 * LANES), f32),
            pltpu.VMEM((4, LANES, LANES), f32),
            pltpu.VMEM((4, 2, LANES, LANES), bf16),
            pltpu.VMEM((4, 2, LANES, LANES), bf16),
            pltpu.VMEM((LANES, LANES), f32),
            pltpu.VMEM((8, LANES), f32),
        ],
    )(core, mine, other, rows)


def do_unpack(rows):
    return call(unpack_kernel, "unpack", (DEPTH, TILE, CELLS), [whole()])(rows)


def exchange(rows, axis, parts):
    shaped = rows.reshape(parts, rows.shape[0] // parts, LANES)
    return lax.all_to_all(shaped, axis, 0, 0).reshape(rows.shape)


def swap_cores(value):
    return lax.ppermute(value, "core", [(0, 1), (1, 0)])


def gram_sum(keep, send):
    depth = SIDES[3]
    half = (keep + swap_cores(send)).reshape(IN_PLANE, NB // IN_PLANE, LANES)
    half = do_sum(lax.all_to_all(half, PLANE, 0, 0), depth, 1.0)
    half = do_sum(lax.all_to_all(half, "z", 0, 0), IN_PLANE, 1.0 / NPTS)
    return lax.all_to_all(half, PLANE, 0, 0).reshape(NB, LANES)


def shards(psi, potential):
    core = lax.axis_index("core").astype(jnp.int32).reshape(1)
    psi, core = lax.optimization_barrier((psi, core))
    bands = exchange(do_pack(jnp.transpose(psi, (1, 0, 2)), potential * (1.0 / HALF_WIDTH)), LAYERS, DOM)
    points = exchange(do_filter(bands), ALL, NB)
    gram = gram_sum(*do_gram(core, points))
    result = exchange(do_solve(core, gram, swap_cores(gram), points), BANDS, BAND)
    return jnp.transpose(do_unpack(result), (1, 0, 2))


def solution(mesh):
    split = Mesh(np.asarray(mesh.devices).reshape(SIDES), NAMES)
    bands = P(BANDS, LAYERS, None)
    return jax.shard_map(
        shards, mesh=split, in_specs=(bands, P(LAYERS, None)), out_specs=bands, check_vma=False
    )
```

```python
import jax
import jax.numpy as jnp
import numpy as np
from jax import lax
from jax.experimental import pallas as pl
from jax.experimental.pallas import tpu as pltpu
from jax.sharding import Mesh, PartitionSpec as P

NB = 512
LX = 32
LY = 16
NZ = 192
CELLS = LX * LY
NPTS = NZ * CELLS
DEG = 4
DOM = 32
BAND = 16
TILE = NB // BAND
DEPTH = NZ // DOM
LANES = 128
SIDES = (8, 2, 2, 8, 2)
NAMES = ("y", "xh", "core", "z", "xl")
LAYERS = ("y", "xh", "core")
BANDS = ("z", "xl")
ALL = BANDS + LAYERS
PLANE = ("xl", "y", "xh")
BACK = ("xl", "z")
IN_PLANE = 32

COEF = (
    -5369.0 / 1800.0,
    12.0 / 7.0,
    -15.0 / 56.0,
    10.0 / 189.0,
    -1.0 / 112.0,
    2.0 / 1925.0,
    -1.0 / 16632.0,
)
INV_SPACING2 = 4.0
CENTRE = 24.0
HALF_WIDTH = 20.0

f32 = jnp.float32
bf16 = jnp.bfloat16


def split_constant(matrix):
    pieces = []
    rest = matrix.astype(np.float64)
    for _ in range(2):
        piece = rest.astype(np.float32).astype(bf16)
        pieces.append(piece)
        rest = rest - piece.astype(np.float64)
    return pieces


def plane_matrix():
    out = np.zeros((CELLS, CELLS))
    scale = -0.5 * INV_SPACING2 / HALF_WIDTH
    for y in range(LY):
        for x in range(LX):
            row = y * LX + x
            out[row, row] += scale * 3.0 * COEF[0] - CENTRE / HALF_WIDTH
            for k in range(1, 7):
                for step in (k, -k):
                    out[row, y * LX + (x + step) % LX] += scale * COEF[k]
                    out[row, (y + step) % LY * LX + x] += scale * COEF[k]
    return out


def layer_matrix():
    out = np.zeros((NZ, NZ))
    scale = -0.5 * INV_SPACING2 / HALF_WIDTH
    for k in range(1, 7):
        out += scale * COEF[k] * (np.eye(NZ, k=k) + np.eye(NZ, k=-k))
    return out


def split_value(value):
    high = value.astype(bf16)
    return high, (value - high.astype(f32)).astype(bf16)


NN = ((1,), (0,))
NT = ((1,), (1,))


def dot_split(left, right, dims):
    a = jnp.concatenate([left[0], left[1], left[0]], axis=dims[0][0])
    b = jnp.concatenate([right[1], right[0], right[0]], axis=dims[1][0])
    return lax.dot_general(a, b, (dims, ((), ())), preferred_element_type=f32)


def dot_apart(left, right):
    def dot(a, b):
        return jnp.dot(a, b, preferred_element_type=f32)

    return (dot(left[0], right[1]) + dot(left[1], right[0])) + dot(left[0], right[0])


def pack_kernel(psi, potential, out):
    for layer in range(DEPTH):
        for quarter in range(4):
            lanes = slice(quarter * LANES, (quarter + 1) * LANES)
            row = layer * 8 + quarter
            out[pl.ds(row, TILE, stride=8 * DEPTH), :] = psi[layer, :, lanes]
            out[pl.ds(row + 4, TILE, stride=8 * DEPTH), :] = jnp.broadcast_to(
                potential[layer : layer + 1, lanes], (TILE, LANES)
            )


def filter_kernel(rows, strip, m_layer, out, scratch, m_plane):
    for piece in range(2):
        for i in range(4):
            for j in range(4):
                at = (j - i) % 4 * LANES
                m_plane[piece, i * LANES : (i + 1) * LANES, j * LANES : (j + 1) * LANES] = strip[
                    piece, :, at : at + LANES
                ]
    start = jnp.concatenate([rows[pl.ds(q, NZ, stride=8), :] for q in range(4)], axis=1)
    potential = jnp.concatenate([rows[pl.ds(4 + q, NZ, stride=8), :] for q in range(4)], axis=1)
    plane = (m_plane[0], m_plane[1])
    layers = (m_layer[0], m_layer[1])

    def apply(values):
        pieces = split_value(values)
        return dot_apart(pieces, plane) + dot_apart(layers, pieces) + potential * values

    previous = start
    current = apply(start)
    for _ in range(1, DEG):
        previous, current = current, 2.0 * apply(current) - previous
    norm = jnp.sum(jnp.sum(current * current, axis=0, keepdims=True), axis=1, keepdims=True) * (
        1.0 / NPTS
    )
    for quarter in range(4):
        scratch[quarter * NZ : (quarter + 1) * NZ, :] = current[
            :, quarter * LANES : (quarter + 1) * LANES
        ]
    lane = lax.broadcasted_iota(jnp.int32, (DOM, LANES), 1)
    norms = jnp.broadcast_to(norm, (DOM, LANES))
    for piece in range(BAND):
        first = scratch[pl.ds((piece % 4) * NZ + piece // 4, DOM, stride=DEPTH), :]
        half = piece // 2
        second = scratch[pl.ds((half % 4) * NZ + 4 + half // 4, DOM, stride=DEPTH), :]
        if piece % 2:
            second = pltpu.roll(second, 64, 1)
        out[pl.ds(piece * 2 * DOM, DOM, stride=2), :] = first
        out[pl.ds(piece * 2 * DOM + 1, DOM, stride=2), :] = jnp.where(lane < 64, second, norms)


def points_of(rows):
    first = rows[pl.ds(0, NB, stride=2), :]
    second = rows[pl.ds(1, NB, stride=2), :]
    lane = lax.broadcasted_iota(jnp.int32, (NB, LANES), 1)
    return first, jnp.where(lane < 64, second, 0.0), second


def gram_kernel(core, rows, keep, send):
    first, second, _ = points_of(rows)
    points = split_value(jnp.concatenate([first, second], axis=1))
    low, high = [p[:256] for p in points], [p[256:] for p in points]
    row = lax.broadcasted_iota(jnp.int32, (256, 256), 0)
    col = lax.broadcasted_iota(jnp.int32, (256, 256), 1)
    folded = jnp.where(col <= row, dot_split(low, low, NT), dot_split(high, high, NT))
    below = dot_split(high, low, NT)
    first = core[0] == 0
    for half in range(2):
        lanes = slice(half * LANES, (half + 1) * LANES)
        at = slice(half * 256, (half + 1) * 256)
        keep[at, :] = jnp.where(first, folded[:, lanes], below[:, lanes])
        send[at, :] = jnp.where(first, below[:, lanes], folded[:, lanes])


def sum_kernel(scale):
    def kernel(parts, out):
        total = jnp.sum(parts[...], axis=0) * scale
        out[...] = jnp.broadcast_to(total[None], out.shape)

    return kernel


def invert_block(m, y_ref, ones, work):
    full = (8, LANES)
    sub = lax.broadcasted_iota(jnp.int32, full, 0)
    lane = lax.broadcasted_iota(jnp.int32, full, 1)

    def row(value, u):
        return jnp.broadcast_to(value[u : u + 1, :], full)

    def column(value, at):
        return jnp.broadcast_to(value[:, at : at + 1], full)

    def total(terms):
        return ((terms[0] + terms[1]) + (terms[2] + terms[3])) + (
            (terms[4] + terms[5]) + (terms[6] + terms[7])
        )

    def later(q, base, inside):
        def update():
            here = slice(8 * q, 8 * q + 8)
            d = m[here, :]
            terms = [
                column(d, base + t) * y_ref[pl.ds(base + t, 8, stride=0), :] for t in range(8)
            ]
            m[here, :] = jnp.where(inside, 0.0, d) + total(terms)

        return update

    def some(calls, steps_left):
        for _ in range(-(-len(calls) // steps_left)):
            calls.pop(0)()

    v = m[0:8, :]
    waiting = []
    for panel in range(16):
        base = 8 * panel
        inside = (lane >= base) & (lane < base + 8)
        a = [column(v, base + t) * ones for t in range(8)]
        v = jnp.where(inside, jnp.where(lane - base == sub, 1.0, 0.0), v)
        v_rows = [row(v, u) for u in range(8)]
        lower = [jnp.zeros(full, f32) for _ in range(7)]
        scale = jnp.zeros(full, f32)
        pivots = [row(a[0], j) for j in range(8)]
        for k in range(8):
            here = sub == k
            ahead = [row(a[k], j) for j in range(k)] + pivots[k:]
            if k == 7:
                masked = [jnp.where(here, 0.0, a[u]) for u in range(7)]
                y = total([masked[u] * v_rows[u] for u in range(7)] + [jnp.zeros(full, f32)])
                rest = v_rows[7] - total(
                    [ahead[u] * v_rows[u] for u in range(7)] + [jnp.zeros(full, f32)]
                )
            root = lax.rsqrt(ahead[k])
            inverse = root * root
            if k < 7:
                pivots = [None] * (k + 1) + [
                    row(a[k + 1], j) - (ahead[k + 1] * ahead[j]) * inverse for j in range(k + 1, 8)
                ]
            for t in range(k):
                lower[t] = jnp.where(here, a[t], lower[t])
            scale = jnp.where(here, root, scale)
            swept = jnp.where(here, -inverse, a[k] * inverse)
            if k < 7:
                for j in range(8):
                    if j != k:
                        a[j] = jnp.where(here, 0.0, a[j]) - swept * ahead[j]
                a[k] = swept
                if k > 0:
                    some(waiting, 7 - k)
            else:
                y = y + swept * rest
        waiting = []
        if panel < 15:
            y_ref[base : base + 8, :] = y
            d = m[base + 8 : base + 16, :]
            terms = [column(d, base + t) * row(y, t) for t in range(8)]
            following = jnp.where(inside, 0.0, d) + total(terms)
            waiting = [later(q, base, inside) for q in range(panel + 2, 16)]
        done = v
        for t in range(7):
            done = done - lower[t] * v_rows[t]
        m[base : base + 8, :] = jnp.where(lane < base + 8, done * scale, 0.0)
        if panel < 15:
            v = following
        some(work, 16 - panel)


def solve_kernel(core, mine, other, rows, out, s_ref, x_ref, blocks, panels, inverses, y_ref, ones_ref):
    first, second, raw = points_of(rows)
    x_ref[:, :LANES] = first
    x_ref[:, LANES:] = second
    ones_ref[...] = jnp.ones((8, LANES), f32)
    swap = core[0] == 0
    folded = jnp.where(swap, mine[...], other[...])
    folded = jnp.concatenate([folded[:256], folded[256:]], axis=1)
    flipped = folded.T
    row = lax.broadcasted_iota(jnp.int32, (256, 256), 0)
    col = lax.broadcasted_iota(jnp.int32, (256, 256), 1)
    low = jnp.where(col <= row, folded, flipped)
    norms = jnp.broadcast_to(raw[256:, LANES - 1 : LANES], (256, 256))
    high = jnp.where(col == row, norms, jnp.where(col > row, folded, flipped))
    s_ref[0, :256, :] = low[:, :LANES]
    s_ref[1, :256, :] = low[:, LANES:]
    s_ref[0, 256:, :] = jnp.where(swap, other[:256, :], mine[:256, :])
    s_ref[1, 256:, :] = jnp.where(swap, other[256:, :], mine[256:, :])
    s_ref[2, 256:, :] = high[:, :LANES]
    s_ref[3, 256:, :] = high[:, LANES:]

    def at(i):
        return slice(i * LANES, (i + 1) * LANES)

    def pieces(ref, i):
        return ref[i, 0], ref[i, 1]

    def put(ref, i, value):
        ref[i, 0], ref[i, 1] = split_value(value)

    def form_panel(j, i):
        put(panels, i, dot_split(split_value(s_ref[j, at(i), :]), pieces(inverses, j), NT))

    def update_s(k, i):
        s_ref[k, at(i), :] = s_ref[k, at(i), :] - dot_split(
            pieces(panels, i), pieces(panels, k), NT
        )

    def solve_x(j):
        x_ref[at(j), :] = dot_split(pieces(inverses, j), split_value(x_ref[at(j), :]), NN)

    def update_x(j, i):
        x_ref[at(i), :] = x_ref[at(i), :] - dot_split(
            pieces(panels, i), split_value(x_ref[at(j), :]), NN
        )

    ones = ones_ref[...]
    work = []
    blocks[0] = s_ref[0, at(0), :]
    for j in range(4):
        invert_block(blocks.at[j], y_ref, ones, work)
        put(inverses, j, blocks[j])
        work = []
        if j < 3:
            form_panel(j, j + 1)
            blocks[j + 1] = s_ref[j + 1, at(j + 1), :] - dot_split(
                pieces(panels, j + 1), pieces(panels, j + 1), NT
            )
            for i in range(j + 2, 4):
                work.append(lambda j=j, i=i: form_panel(j, i))
                work.append(lambda k=j + 1, i=i: update_s(k, i))
            for k in range(j + 2, 4):
                for i in range(k, 4):
                    work.append(lambda k=k, i=i: update_s(k, i))
        work.append(lambda j=j: solve_x(j))
        for i in range(j + 1, 4):
            work.append(lambda j=j, i=i: update_x(j, i))
    for call_ in work:
        call_()
    for tile in range(BAND):
        at_ = tile * TILE
        to = place(tile) * 48
        out[to : to + 32, :] = x_ref[at_ : at_ + TILE, :LANES]
        out[to + 32 : to + 48, :] = x_ref[at_ : at_ + 16, LANES:] + pltpu.roll(
            x_ref[at_ + 16 : at_ + 32, LANES:], 64, 1
        )


def place(tile):
    return (tile % 2) * (BAND // 2) + tile // 2


def unpack_kernel(rows, out):
    for piece in range(BAND):
        quarter = piece % 4
        out[piece // 4, :, quarter * LANES : (quarter + 1) * LANES] = rows[
            place(piece) * 48 : place(piece) * 48 + 32, :
        ]
    lower = lax.broadcasted_iota(jnp.int32, (16, LANES), 1) < 64
    for half in range(8):
        lanes = slice((half % 4) * LANES, (half % 4 + 1) * LANES)
        even, odd = (
            rows[place(piece) * 48 + 32 : place(piece) * 48 + 48, :]
            for piece in (2 * half, 2 * half + 1)
        )
        out[4 + half // 4, 0:16, lanes] = jnp.where(lower, even, pltpu.roll(odd, 64, 1))
        out[4 + half // 4, 16:32, lanes] = jnp.where(lower, pltpu.roll(even, 64, 1), odd)


def whole():
    return pl.BlockSpec(memory_space=pltpu.VMEM)


def scalar():
    return pl.BlockSpec(memory_space=pltpu.SMEM)


def call(kernel, name, shape, specs, scratch=()):
    return pl.pallas_call(
        kernel,
        name=name,
        out_shape=jax.ShapeDtypeStruct(shape, f32),
        in_specs=specs,
        out_specs=whole(),
        scratch_shapes=list(scratch),
        compiler_params=pltpu.CompilerParams(vmem_limit_bytes=48 << 20),
    )


def do_pack(psi, potential):
    return call(pack_kernel, "pack", (TILE * 8 * DEPTH, LANES), [whole()] * 2)(psi, potential)


def do_filter(rows):
    strip = np.stack(split_constant(plane_matrix()[:LANES]))
    layers = np.stack(split_constant(layer_matrix()))
    return call(
        filter_kernel,
        "filter",
        (2 * NB, LANES),
        [whole()] * 3,
        [pltpu.VMEM((4 * NZ, LANES), f32), pltpu.VMEM((2, CELLS, CELLS), bf16)],
    )(rows, jnp.asarray(strip), jnp.asarray(layers))


def do_gram(core, rows):
    half = jax.ShapeDtypeStruct((NB, LANES), f32)
    return pl.pallas_call(
        gram_kernel,
        name="gram",
        out_shape=(half, half),
        in_specs=[scalar(), whole()],
        out_specs=(whole(), whole()),
        compiler_params=pltpu.CompilerParams(vmem_limit_bytes=48 << 20),
    )(core, rows)


def do_sum(parts, copies, scale):
    return call(sum_kernel(scale), "sum", (copies,) + parts.shape[1:], [whole()])(parts)


def do_solve(core, mine, other, rows):
    return call(
        solve_kernel,
        "solve",
        (BAND * 48, LANES),
        [scalar(), whole(), whole(), whole()],
        [
            pltpu.VMEM((4, NB, LANES), f32),
            pltpu.VMEM((NB, 2 * LANES), f32),
            pltpu.VMEM((4, LANES, LANES), f32),
            pltpu.VMEM((4, 2, LANES, LANES), bf16),
            pltpu.VMEM((4, 2, LANES, LANES), bf16),
            pltpu.VMEM((LANES, LANES), f32),
            pltpu.VMEM((8, LANES), f32),
        ],
    )(core, mine, other, rows)


def do_unpack(rows):
    return call(unpack_kernel, "unpack", (DEPTH, TILE, CELLS), [whole()])(rows)


def exchange(rows, axis, parts):
    shaped = rows.reshape(parts, rows.shape[0] // parts, LANES)
    return lax.all_to_all(shaped, axis, 0, 0).reshape(rows.shape)


def swap_cores(value):
    return lax.ppermute(value, "core", [(0, 1), (1, 0)])


def gram_sum(keep, send):
    depth = SIDES[3]
    half = (keep + swap_cores(send)).reshape(IN_PLANE, NB // IN_PLANE, LANES)
    half = do_sum(lax.all_to_all(half, PLANE, 0, 0), depth, 1.0)
    half = do_sum(lax.all_to_all(half, "z", 0, 0), IN_PLANE, 1.0 / NPTS)
    return lax.all_to_all(half, PLANE, 0, 0).reshape(NB, LANES)


def shards(psi, potential):
    core = lax.axis_index("core").astype(jnp.int32).reshape(1)
    psi, core = lax.optimization_barrier((psi, core))
    bands = exchange(do_pack(jnp.transpose(psi, (1, 0, 2)), potential * (1.0 / HALF_WIDTH)), LAYERS, DOM)
    points = exchange(do_filter(bands), ALL, NB)
    gram = gram_sum(*do_gram(core, points))
    result = exchange(do_solve(core, gram, swap_cores(gram), points), BACK, BAND)
    return jnp.transpose(do_unpack(result), (1, 0, 2))


def solution(mesh):
    split = Mesh(np.asarray(mesh.devices).reshape(SIDES), NAMES)
    bands = P(BANDS, LAYERS, None)
    return jax.shard_map(
        shards, mesh=split, in_specs=(bands, P(LAYERS, None)), out_specs=bands, check_vma=False
    )
```

```python
import jax
import jax.numpy as jnp
import numpy as np
from jax import lax
from jax.experimental import pallas as pl
from jax.experimental.pallas import tpu as pltpu
from jax.sharding import Mesh, PartitionSpec as P

NB = 512
LX = 32
LY = 16
NZ = 192
CELLS = LX * LY
NPTS = NZ * CELLS
DEG = 4
DOM = 32
BAND = 16
TILE = NB // BAND
DEPTH = NZ // DOM
LANES = 128
SIDES = (8, 2, 2, 8, 2)
NAMES = ("y", "xh", "core", "z", "xl")
LAYERS = ("y", "xh", "core")
BANDS = ("z", "xl")
ALL = BANDS + LAYERS
PLANE = ("y", "xh", "xl")
BACK = ("xl", "z")
IN_PLANE = 32

COEF = (
    -5369.0 / 1800.0,
    12.0 / 7.0,
    -15.0 / 56.0,
    10.0 / 189.0,
    -1.0 / 112.0,
    2.0 / 1925.0,
    -1.0 / 16632.0,
)
INV_SPACING2 = 4.0
CENTRE = 24.0
HALF_WIDTH = 20.0

f32 = jnp.float32
bf16 = jnp.bfloat16


def split_constant(matrix):
    pieces = []
    rest = matrix.astype(np.float64)
    for _ in range(2):
        piece = rest.astype(np.float32).astype(bf16)
        pieces.append(piece)
        rest = rest - piece.astype(np.float64)
    return pieces


def plane_matrix():
    out = np.zeros((CELLS, CELLS))
    scale = -0.5 * INV_SPACING2 / HALF_WIDTH
    for y in range(LY):
        for x in range(LX):
            row = y * LX + x
            out[row, row] += scale * 3.0 * COEF[0] - CENTRE / HALF_WIDTH
            for k in range(1, 7):
                for step in (k, -k):
                    out[row, y * LX + (x + step) % LX] += scale * COEF[k]
                    out[row, (y + step) % LY * LX + x] += scale * COEF[k]
    return out


def layer_matrix():
    out = np.zeros((NZ, NZ))
    scale = -0.5 * INV_SPACING2 / HALF_WIDTH
    for k in range(1, 7):
        out += scale * COEF[k] * (np.eye(NZ, k=k) + np.eye(NZ, k=-k))
    return out


def split_value(value):
    high = value.astype(bf16)
    return high, (value - high.astype(f32)).astype(bf16)


NN = ((1,), (0,))
NT = ((1,), (1,))


def dot_split(left, right, dims):
    a = jnp.concatenate([left[0], left[1], left[0]], axis=dims[0][0])
    b = jnp.concatenate([right[1], right[0], right[0]], axis=dims[1][0])
    return lax.dot_general(a, b, (dims, ((), ())), preferred_element_type=f32)


def dot_apart(left, right):
    def dot(a, b):
        return jnp.dot(a, b, preferred_element_type=f32)

    return (dot(left[0], right[1]) + dot(left[1], right[0])) + dot(left[0], right[0])


def pack_kernel(psi, potential, out):
    for layer in range(DEPTH):
        for quarter in range(4):
            lanes = slice(quarter * LANES, (quarter + 1) * LANES)
            row = layer * 8 + quarter
            out[pl.ds(row, TILE, stride=8 * DEPTH), :] = psi[layer, :, lanes]
            out[pl.ds(row + 4, TILE, stride=8 * DEPTH), :] = jnp.broadcast_to(
                potential[layer : layer + 1, lanes], (TILE, LANES)
            )


def filter_kernel(rows, strip, m_layer, out, scratch, m_plane):
    for piece in range(2):
        for i in range(4):
            for j in range(4):
                at = (j - i) % 4 * LANES
                m_plane[piece, i * LANES : (i + 1) * LANES, j * LANES : (j + 1) * LANES] = strip[
                    piece, :, at : at + LANES
                ]
    start = jnp.concatenate([rows[pl.ds(q, NZ, stride=8), :] for q in range(4)], axis=1)
    potential = jnp.concatenate([rows[pl.ds(4 + q, NZ, stride=8), :] for q in range(4)], axis=1)
    plane = (m_plane[0], m_plane[1])
    layers = (m_layer[0], m_layer[1])

    def apply(values):
        pieces = split_value(values)
        return dot_apart(pieces, plane) + dot_apart(layers, pieces) + potential * values

    previous = start
    current = apply(start)
    for _ in range(1, DEG):
        previous, current = current, 2.0 * apply(current) - previous
    norm = jnp.sum(jnp.sum(current * current, axis=0, keepdims=True), axis=1, keepdims=True) * (
        1.0 / NPTS
    )
    for quarter in range(4):
        scratch[quarter * NZ : (quarter + 1) * NZ, :] = current[
            :, quarter * LANES : (quarter + 1) * LANES
        ]
    lane = lax.broadcasted_iota(jnp.int32, (DOM, LANES), 1)
    norms = jnp.broadcast_to(norm, (DOM, LANES))
    for piece in range(BAND):
        first = scratch[pl.ds((piece % 4) * NZ + piece // 4, DOM, stride=DEPTH), :]
        half = piece // 2
        second = scratch[pl.ds((half % 4) * NZ + 4 + half // 4, DOM, stride=DEPTH), :]
        if piece % 2:
            second = pltpu.roll(second, 64, 1)
        out[pl.ds(piece * 2 * DOM, DOM, stride=2), :] = first
        out[pl.ds(piece * 2 * DOM + 1, DOM, stride=2), :] = jnp.where(lane < 64, second, norms)


def points_of(rows):
    first = rows[pl.ds(0, NB, stride=2), :]
    second = rows[pl.ds(1, NB, stride=2), :]
    lane = lax.broadcasted_iota(jnp.int32, (NB, LANES), 1)
    return first, jnp.where(lane < 64, second, 0.0), second


def gram_kernel(core, rows, keep, send):
    first, second, _ = points_of(rows)
    points = split_value(jnp.concatenate([first, second], axis=1))
    low, high = [p[:256] for p in points], [p[256:] for p in points]
    row = lax.broadcasted_iota(jnp.int32, (256, 256), 0)
    col = lax.broadcasted_iota(jnp.int32, (256, 256), 1)
    folded = jnp.where(col <= row, dot_split(low, low, NT), dot_split(high, high, NT))
    below = dot_split(high, low, NT)
    first = core[0] == 0
    for half in range(2):
        lanes = slice(half * LANES, (half + 1) * LANES)
        at = slice(half * 256, (half + 1) * 256)
        keep[at, :] = jnp.where(first, folded[:, lanes], below[:, lanes])
        send[at, :] = jnp.where(first, below[:, lanes], folded[:, lanes])


def sum_kernel(scale):
    def kernel(parts, out):
        total = jnp.sum(parts[...], axis=0) * scale
        out[...] = jnp.broadcast_to(total[None], out.shape)

    return kernel


def invert_block(m, y_ref, ones, work):
    full = (8, LANES)
    sub = lax.broadcasted_iota(jnp.int32, full, 0)
    lane = lax.broadcasted_iota(jnp.int32, full, 1)

    def row(value, u):
        return jnp.broadcast_to(value[u : u + 1, :], full)

    def column(value, at):
        return jnp.broadcast_to(value[:, at : at + 1], full)

    def total(terms):
        return ((terms[0] + terms[1]) + (terms[2] + terms[3])) + (
            (terms[4] + terms[5]) + (terms[6] + terms[7])
        )

    def later(q, base, inside):
        def update():
            here = slice(8 * q, 8 * q + 8)
            d = m[here, :]
            terms = [
                column(d, base + t) * y_ref[pl.ds(base + t, 8, stride=0), :] for t in range(8)
            ]
            m[here, :] = jnp.where(inside, 0.0, d) + total(terms)

        return update

    def some(calls, steps_left):
        for _ in range(-(-len(calls) // steps_left)):
            calls.pop(0)()

    v = m[0:8, :]
    waiting = []
    for panel in range(16):
        base = 8 * panel
        inside = (lane >= base) & (lane < base + 8)
        a = [column(v, base + t) * ones for t in range(8)]
        v = jnp.where(inside, jnp.where(lane - base == sub, 1.0, 0.0), v)
        v_rows = [row(v, u) for u in range(8)]
        lower = [jnp.zeros(full, f32) for _ in range(7)]
        scale = jnp.zeros(full, f32)
        pivots = [row(a[0], j) for j in range(8)]
        for k in range(8):
            here = sub == k
            ahead = [row(a[k], j) for j in range(k)] + pivots[k:]
            if k == 7:
                masked = [jnp.where(here, 0.0, a[u]) for u in range(7)]
                y = total([masked[u] * v_rows[u] for u in range(7)] + [jnp.zeros(full, f32)])
                rest = v_rows[7] - total(
                    [ahead[u] * v_rows[u] for u in range(7)] + [jnp.zeros(full, f32)]
                )
            root = lax.rsqrt(ahead[k])
            inverse = root * root
            if k < 7:
                pivots = [None] * (k + 1) + [
                    row(a[k + 1], j) - (ahead[k + 1] * ahead[j]) * inverse for j in range(k + 1, 8)
                ]
            for t in range(k):
                lower[t] = jnp.where(here, a[t], lower[t])
            scale = jnp.where(here, root, scale)
            swept = jnp.where(here, -inverse, a[k] * inverse)
            if k < 7:
                for j in range(8):
                    if j != k:
                        a[j] = jnp.where(here, 0.0, a[j]) - swept * ahead[j]
                a[k] = swept
                if k > 0:
                    some(waiting, 7 - k)
            else:
                y = y + swept * rest
        waiting = []
        if panel < 15:
            y_ref[base : base + 8, :] = y
            d = m[base + 8 : base + 16, :]
            terms = [column(d, base + t) * row(y, t) for t in range(8)]
            following = jnp.where(inside, 0.0, d) + total(terms)
            waiting = [later(q, base, inside) for q in range(panel + 2, 16)]
        done = v
        for t in range(7):
            done = done - lower[t] * v_rows[t]
        m[base : base + 8, :] = jnp.where(lane < base + 8, done * scale, 0.0)
        if panel < 15:
            v = following
        some(work, 16 - panel)


def solve_kernel(core, mine, other, rows, out, s_ref, x_ref, blocks, panels, inverses, y_ref, ones_ref):
    first, second, raw = points_of(rows)
    x_ref[:, :LANES] = first
    x_ref[:, LANES:] = second
    ones_ref[...] = jnp.ones((8, LANES), f32)
    swap = core[0] == 0
    folded = jnp.where(swap, mine[...], other[...])
    folded = jnp.concatenate([folded[:256], folded[256:]], axis=1)
    flipped = folded.T
    row = lax.broadcasted_iota(jnp.int32, (256, 256), 0)
    col = lax.broadcasted_iota(jnp.int32, (256, 256), 1)
    low = jnp.where(col <= row, folded, flipped)
    norms = jnp.broadcast_to(raw[256:, LANES - 1 : LANES], (256, 256))
    high = jnp.where(col == row, norms, jnp.where(col > row, folded, flipped))
    s_ref[0, :256, :] = low[:, :LANES]
    s_ref[1, :256, :] = low[:, LANES:]
    s_ref[0, 256:, :] = jnp.where(swap, other[:256, :], mine[:256, :])
    s_ref[1, 256:, :] = jnp.where(swap, other[256:, :], mine[256:, :])
    s_ref[2, 256:, :] = high[:, :LANES]
    s_ref[3, 256:, :] = high[:, LANES:]

    def at(i):
        return slice(i * LANES, (i + 1) * LANES)

    def pieces(ref, i):
        return ref[i, 0], ref[i, 1]

    def put(ref, i, value):
        ref[i, 0], ref[i, 1] = split_value(value)

    def form_panel(j, i):
        put(panels, i, dot_split(split_value(s_ref[j, at(i), :]), pieces(inverses, j), NT))

    def update_s(k, i):
        s_ref[k, at(i), :] = s_ref[k, at(i), :] - dot_split(
            pieces(panels, i), pieces(panels, k), NT
        )

    def solve_x(j):
        x_ref[at(j), :] = dot_split(pieces(inverses, j), split_value(x_ref[at(j), :]), NN)

    def update_x(j, i):
        x_ref[at(i), :] = x_ref[at(i), :] - dot_split(
            pieces(panels, i), split_value(x_ref[at(j), :]), NN
        )

    ones = ones_ref[...]
    work = []
    blocks[0] = s_ref[0, at(0), :]
    for j in range(4):
        invert_block(blocks.at[j], y_ref, ones, work)
        put(inverses, j, blocks[j])
        work = []
        if j < 3:
            form_panel(j, j + 1)
            blocks[j + 1] = s_ref[j + 1, at(j + 1), :] - dot_split(
                pieces(panels, j + 1), pieces(panels, j + 1), NT
            )
            for i in range(j + 2, 4):
                work.append(lambda j=j, i=i: form_panel(j, i))
                work.append(lambda k=j + 1, i=i: update_s(k, i))
            for k in range(j + 2, 4):
                for i in range(k, 4):
                    work.append(lambda k=k, i=i: update_s(k, i))
        work.append(lambda j=j: solve_x(j))
        for i in range(j + 1, 4):
            work.append(lambda j=j, i=i: update_x(j, i))
    for call_ in work:
        call_()
    for tile in range(BAND):
        at_ = tile * TILE
        to = place(tile) * 48
        out[to : to + 32, :] = x_ref[at_ : at_ + TILE, :LANES]
        out[to + 32 : to + 48, :] = x_ref[at_ : at_ + 16, LANES:] + pltpu.roll(
            x_ref[at_ + 16 : at_ + 32, LANES:], 64, 1
        )


def place(tile):
    return (tile % 2) * (BAND // 2) + tile // 2


def unpack_kernel(rows, out):
    for piece in range(BAND):
        quarter = piece % 4
        out[piece // 4, :, quarter * LANES : (quarter + 1) * LANES] = rows[
            place(piece) * 48 : place(piece) * 48 + 32, :
        ]
    lower = lax.broadcasted_iota(jnp.int32, (16, LANES), 1) < 64
    for half in range(8):
        lanes = slice((half % 4) * LANES, (half % 4 + 1) * LANES)
        even, odd = (
            rows[place(piece) * 48 + 32 : place(piece) * 48 + 48, :]
            for piece in (2 * half, 2 * half + 1)
        )
        out[4 + half // 4, 0:16, lanes] = jnp.where(lower, even, pltpu.roll(odd, 64, 1))
        out[4 + half // 4, 16:32, lanes] = jnp.where(lower, pltpu.roll(even, 64, 1), odd)


def whole():
    return pl.BlockSpec(memory_space=pltpu.VMEM)


def scalar():
    return pl.BlockSpec(memory_space=pltpu.SMEM)


def call(kernel, name, shape, specs, scratch=()):
    return pl.pallas_call(
        kernel,
        name=name,
        out_shape=jax.ShapeDtypeStruct(shape, f32),
        in_specs=specs,
        out_specs=whole(),
        scratch_shapes=list(scratch),
        compiler_params=pltpu.CompilerParams(vmem_limit_bytes=48 << 20),
    )


def do_pack(psi, potential):
    return call(pack_kernel, "pack", (TILE * 8 * DEPTH, LANES), [whole()] * 2)(psi, potential)


def do_filter(rows):
    strip = np.stack(split_constant(plane_matrix()[:LANES]))
    layers = np.stack(split_constant(layer_matrix()))
    return call(
        filter_kernel,
        "filter",
        (2 * NB, LANES),
        [whole()] * 3,
        [pltpu.VMEM((4 * NZ, LANES), f32), pltpu.VMEM((2, CELLS, CELLS), bf16)],
    )(rows, jnp.asarray(strip), jnp.asarray(layers))


def do_gram(core, rows):
    half = jax.ShapeDtypeStruct((NB, LANES), f32)
    return pl.pallas_call(
        gram_kernel,
        name="gram",
        out_shape=(half, half),
        in_specs=[scalar(), whole()],
        out_specs=(whole(), whole()),
        compiler_params=pltpu.CompilerParams(vmem_limit_bytes=48 << 20),
    )(core, rows)


def do_sum(parts, copies, scale):
    return call(sum_kernel(scale), "sum", (copies,) + parts.shape[1:], [whole()])(parts)


def do_solve(core, mine, other, rows):
    return call(
        solve_kernel,
        "solve",
        (BAND * 48, LANES),
        [scalar(), whole(), whole(), whole()],
        [
            pltpu.VMEM((4, NB, LANES), f32),
            pltpu.VMEM((NB, 2 * LANES), f32),
            pltpu.VMEM((4, LANES, LANES), f32),
            pltpu.VMEM((4, 2, LANES, LANES), bf16),
            pltpu.VMEM((4, 2, LANES, LANES), bf16),
            pltpu.VMEM((LANES, LANES), f32),
            pltpu.VMEM((8, LANES), f32),
        ],
    )(core, mine, other, rows)


def do_unpack(rows):
    return call(unpack_kernel, "unpack", (DEPTH, TILE, CELLS), [whole()])(rows)


def exchange(rows, axis, parts):
    shaped = rows.reshape(parts, rows.shape[0] // parts, LANES)
    return lax.all_to_all(shaped, axis, 0, 0).reshape(rows.shape)


def swap_cores(value):
    return lax.ppermute(value, "core", [(0, 1), (1, 0)])


def gram_sum(keep, send):
    depth = SIDES[3]
    half = (keep + swap_cores(send)).reshape(IN_PLANE, NB // IN_PLANE, LANES)
    half = do_sum(lax.all_to_all(half, PLANE, 0, 0), depth, 1.0)
    half = do_sum(lax.all_to_all(half, "z", 0, 0), IN_PLANE, 1.0 / NPTS)
    return lax.all_to_all(half, PLANE, 0, 0).reshape(NB, LANES)


def shards(psi, potential):
    core = lax.axis_index("core").astype(jnp.int32).reshape(1)
    psi, core = lax.optimization_barrier((psi, core))
    bands = exchange(do_pack(jnp.transpose(psi, (1, 0, 2)), potential * (1.0 / HALF_WIDTH)), LAYERS, DOM)
    points = exchange(do_filter(bands), ALL, NB)
    gram = gram_sum(*do_gram(core, points))
    result = exchange(do_solve(core, gram, swap_cores(gram), points), BACK, BAND)
    return jnp.transpose(do_unpack(result), (1, 0, 2))


def solution(mesh):
    split = Mesh(np.asarray(mesh.devices).reshape(SIDES), NAMES)
    bands = P(BANDS, LAYERS, None)
    return jax.shard_map(
        shards, mesh=split, in_specs=(bands, P(LAYERS, None)), out_specs=bands, check_vma=False
    )
```
